32 devices in a mesh: expert: 8 (over z, core), fsdp: 4 (over y, x).
Axes of the slice: x: 2, y: 2, z: 4, core: 2. Of those that a mesh axis runs over, the one named last changes fastest.
Arguments:
- tokens: bfloat16 [256, 4096], P('expert', 'fsdp'), may hold values from -6 to 6
- cotangent: bfloat16 [256, 4096], P('expert', 'fsdp'), may hold values from -6 to 6
- expert_ids: int32 [256, 8], P('expert'), may hold values from 0 to 7, as said below
- gate_logits: float32 [256, 8], P('expert'), may hold values from -6 to 6
- shadow_plan: int32 [8], replicated, may hold values from 0 to 1, as said below
- w_in: bfloat16 [8, 4096, 2, 768], P('expert', 'fsdp'), may hold values from -0.09375 to 0.09375
- w_out: bfloat16 [8, 768, 4096], P('expert', None, 'fsdp'), may hold values from -0.21875 to 0.21875
- mom_in: bfloat16 [8, 4096, 2, 768], P('expert', 'fsdp'), may hold values from -3 to 3
- mom_out: bfloat16 [8, 768, 4096], P('expert', None, 'fsdp'), may hold values from -3 to 3
- in_rows: float32 [8, 2, 4096], P('expert', None, 'fsdp'), may hold values from 1e-05 to 0.01
- in_cols: float32 [8, 2, 2, 768], P('expert'), may hold values from 1e-05 to 0.01
- out_rows: float32 [8, 2, 768], P('expert'), may hold values from 1e-05 to 0.01
- out_cols: float32 [8, 2, 4096], P('expert', None, 'fsdp'), may hold values from 1e-05 to 0.01
Outputs:
- output: bfloat16 [256, 4096], P('expert', 'fsdp')
- grad_tokens: bfloat16 [256, 4096], P('expert', 'fsdp')
- new_w_in: bfloat16 [8, 4096, 2, 768], P('expert', 'fsdp')
- new_w_out: bfloat16 [8, 768, 4096], P('expert', None, 'fsdp')
- new_mom_in: bfloat16 [8, 4096, 2, 768], P('expert', 'fsdp')
- new_mom_out: bfloat16 [8, 768, 4096], P('expert', None, 'fsdp')
- new_in_rows: float32 [8, 2, 4096], P('expert', None, 'fsdp')
- new_in_cols: float32 [8, 2, 2, 768], P('expert')
- new_out_rows: float32 [8, 2, 768], P('expert')
- new_out_cols: float32 [8, 2, 4096], P('expert', None, 'fsdp')
The draws below stay inside these ranges and needn't reach their ends.
Inputs may be any that keep to these rules, and one draw needn't show every extreme that they name: `expert_ids`: each row names 8 different experts. `shadow_plan`: exactly 1 entries are 1, one in every run of 8 consecutive experts starting at expert 0, all at the same position within their run; the others 0.
All inputs are finite; a program needn't handle non-finite values.
Results may differ from the reference program's by a relative error of at most 0.0064.
Values may be sent and summed in bfloat16 or wider, within the bound.
No kernel may reach another device: no remote copies, remote signals or barrier semaphores. Data moves between devices by JAX's collectives and lax.ppermute only.
A program may use at most 128 MiB of HBM per device.

```python
import math
from functools import partial
import jax
import jax.numpy as jnp
from jax import lax

D = 4096
FF = 768
TOPK = 8
TOK_DEV = 32
EXPERTS = 8
TOKENS = 256
N_EXPERT = 8


def hot_experts(key):
    start = jax.random.randint(jax.random.fold_in(key, 11), (), 0, 8)
    return (jnp.arange(EXPERTS, dtype=jnp.int32) % 8 == start).astype(jnp.int32)


def draw_expert_ids(key, part):
    marked = hot_experts(key)
    token_noise = jax.random.randint(jax.random.fold_in(key, 23), (TOKENS, EXPERTS), 0, 65536)
    expert_bias = jax.random.randint(jax.random.fold_in(key, 29), (EXPERTS,), 0, 16384)
    scores = (token_noise + expert_bias[None, :] + marked[None, :] * 32768) * EXPERTS + jnp.arange(EXPERTS, dtype=jnp.int32)[None, :]
    chosen = lax.top_k(scores, TOPK)[1]
    return chosen.astype(jnp.int32)


def draw_shadow_plan(key, part):
    return hot_experts(key)


def block_levels(key, dims, cuts, least, top_value):
    gain, own = 1.0, jax.random.fold_in(key, 6)
    for dim, shards_of in cuts:
        steps = jnp.exp(jax.random.uniform(jax.random.fold_in(own, dim), (shards_of,), jnp.float32, least / len(cuts), top_value / len(cuts)))
        gain = gain * jnp.repeat(steps, dims[dim] // shards_of).reshape([-1 if axis == dim else 1 for axis in range(len(dims))])
    return gain


def gaussian(rng, dims, spread, limit, shards=(), kind=jnp.bfloat16):
    entries = spread * jax.random.normal(rng, dims, jnp.float32)
    if shards:
        entries = entries * block_levels(rng, dims, shards, -0.22, 0.18)
    return jnp.clip(entries, -limit, limit).astype(kind)


def setup_inputs(seed: int = 0) -> dict:
    streams_of = jax.random.split(jax.random.key(seed), 14)
    tokens = gaussian(streams_of[0], (TOKENS, D), 1.0, 6.0, ((0, 8), (1, 4)))
    cotangent = gaussian(streams_of[1], (TOKENS, D), 1.0, 6.0, ((0, 8), (1, 4)))
    expert_ids = draw_expert_ids(jax.random.fold_in(streams_of[13], 71), 0)
    gate_logits = gaussian(streams_of[3], (TOKENS, TOPK), 1.5, 6.0, ((0, 8),), jnp.float32)
    shadow_plan = draw_shadow_plan(jax.random.fold_in(streams_of[13], 71), 0)
    w_in = gaussian(streams_of[5], (EXPERTS, D, 2, FF), D ** -0.5, 0.09375, ((0, 8), (1, 4)))
    w_out = gaussian(streams_of[6], (EXPERTS, FF, D), FF ** -0.5, 0.21875, ((0, 8), (2, 4)))
    mom_in = gaussian(streams_of[7], (EXPERTS, D, 2, FF), 0.3, 3.0, ((0, 8), (1, 4)))
    mom_out = gaussian(streams_of[8], (EXPERTS, FF, D), 0.3, 3.0, ((0, 8), (2, 4)))
    in_rows = jnp.clip(jnp.exp(math.log(0.01) - 6.9077553 * jax.random.uniform(streams_of[9], (EXPERTS, 2, D), jnp.float32) ** block_levels(streams_of[9], (EXPERTS, 2, D), ((0, 8), (2, 4)), -0.2, 0.2)), 9.999999747378752e-06, 0.01)
    in_cols = jnp.clip(jnp.exp(math.log(0.01) - 6.9077553 * jax.random.uniform(streams_of[10], (EXPERTS, 2, 2, FF), jnp.float32) ** block_levels(streams_of[10], (EXPERTS, 2, 2, FF), ((0, 8),), -0.2, 0.2)), 9.999999747378752e-06, 0.01)
    out_rows = jnp.clip(jnp.exp(math.log(0.01) - 6.9077553 * jax.random.uniform(streams_of[11], (EXPERTS, 2, FF), jnp.float32) ** block_levels(streams_of[11], (EXPERTS, 2, FF), ((0, 8),), -0.2, 0.2)), 9.999999747378752e-06, 0.01)
    out_cols = jnp.clip(jnp.exp(math.log(0.01) - 6.9077553 * jax.random.uniform(streams_of[12], (EXPERTS, 2, D), jnp.float32) ** block_levels(streams_of[12], (EXPERTS, 2, D), ((0, 8), (2, 4)), -0.2, 0.2)), 9.999999747378752e-06, 0.01)
    return {"tokens": tokens, "cotangent": cotangent, "expert_ids": expert_ids, "gate_logits": gate_logits, "shadow_plan": shadow_plan, "w_in": w_in, "w_out": w_out, "mom_in": mom_in, "mom_out": mom_out, "in_rows": in_rows, "in_cols": in_cols, "out_rows": out_rows, "out_cols": out_cols}


BETA_ONE = 0.9
BETA_TWO = 0.999
BETA_THREE = 0.9999
EPS_ONE = 1e-30
EPS_TWO = 1e-16
CLIP_LIMIT = 1.0
LEARN_RATE = 0.01

def slot_plan(expert_ids, shadow_plan, capacity):
    flat_ids = expert_ids.reshape(-1).astype(jnp.int32)
    expert_count = shadow_plan.shape[0]
    one_hot = (flat_ids[:, None] == jnp.arange(expert_count, dtype=jnp.int32)[None, :]).astype(jnp.int32)
    earlier = (jnp.cumsum(one_hot, axis=0) - one_hot).astype(jnp.int32)
    slot_rank = lax.optimization_barrier(jnp.sum(earlier * one_hot, axis=1)).astype(jnp.int32)
    is_hot = lax.optimization_barrier(jnp.sum(one_hot * shadow_plan[None, :], axis=1)).astype(jnp.int32)
    kept_mask = (slot_rank < capacity) | (is_hot > 0) & (slot_rank < 2 * capacity)
    return (flat_ids, slot_rank, kept_mask)

def came_step(gradient, weight, moment, row_state, col_state):
    squares = gradient * gradient + EPS_ONE
    row_v = BETA_TWO * row_state[0] + (1.0 - BETA_TWO) * lax.optimization_barrier(jnp.mean(squares, axis=1))
    col_v = BETA_TWO * col_state[0] + (1.0 - BETA_TWO) * lax.optimization_barrier(jnp.mean(squares, axis=0))
    scaled = gradient / jnp.sqrt(row_v[:, None] * col_v[None, :] / jnp.mean(row_v))
    scaled = scaled / jnp.maximum(1.0, jnp.sqrt(jnp.mean(scaled * scaled)) / CLIP_LIMIT)
    moment_new = BETA_ONE * moment.astype(jnp.float32) + (1.0 - BETA_ONE) * scaled
    residue = (scaled - moment_new) * (scaled - moment_new) + EPS_TWO
    row_r = BETA_THREE * row_state[1] + (1.0 - BETA_THREE) * lax.optimization_barrier(jnp.mean(residue, axis=1))
    col_r = BETA_THREE * col_state[1] + (1.0 - BETA_THREE) * lax.optimization_barrier(jnp.mean(residue, axis=0))
    stepped = moment_new / jnp.sqrt(row_r[:, None] * col_r[None, :] / jnp.mean(row_r))
    weight_new = (weight.astype(jnp.float32) - LEARN_RATE * stepped).astype(jnp.bfloat16)
    return (weight_new, moment_new.astype(jnp.bfloat16), jnp.stack([row_v, row_r]), jnp.stack([col_v, col_r]))

def reference(tokens, cotangent, expert_ids, gate_logits, shadow_plan, w_in, w_out, mom_in, mom_out, in_rows, in_cols, out_rows, out_cols):
    capacity = TOK_DEV * TOPK // N_EXPERT
    slots = 2 * capacity
    block_slots = N_EXPERT * slots
    grouped = expert_ids.reshape(N_EXPERT, TOK_DEV, TOPK)
    flat_ids, slot_rank, kept_mask = jax.vmap(partial(slot_plan, shadow_plan=shadow_plan, capacity=capacity))(grouped)
    source_index = jnp.arange(N_EXPERT, dtype=jnp.int32)[:, None]
    slot_index = jnp.where(kept_mask, flat_ids * block_slots + source_index * slots + slot_rank, EXPERTS * block_slots).reshape(-1).astype(jnp.int32)
    token_index = (jnp.arange(TOKENS * TOPK, dtype=jnp.int32) // TOPK).astype(jnp.int32)
    slot_token = jnp.full((EXPERTS * block_slots,), TOKENS, jnp.int32).at[slot_index].set(token_index, mode='drop').reshape(EXPERTS, block_slots)
    sig_logits = jax.nn.sigmoid(gate_logits)
    gates = sig_logits / lax.optimization_barrier(jnp.sum(sig_logits, axis=1, keepdims=True))
    pair_gate = jnp.where(kept_mask.reshape(-1), gates.reshape(-1), jnp.zeros_like(gates.reshape(-1)))
    slot_gate = jnp.zeros((EXPERTS * block_slots,), jnp.float32).at[slot_index].set(pair_gate, mode='drop').reshape(EXPERTS, block_slots)
    zero_row = jnp.zeros((1, D), jnp.bfloat16)
    token_table = jnp.concatenate([tokens, zero_row], axis=0)
    cot_table = jnp.concatenate([cotangent, zero_row], axis=0)

    def expert_step(totals, inputs):
        out_total, grad_total = totals
        weight_in, weight_out, moment_in, moment_out, rows_in, cols_in, rows_out, cols_out, token_ids, slot_weights = inputs
        slot_rows = token_table[token_ids]
        flat_in = weight_in.reshape(D, 2 * FF)
        gate_up = jnp.dot(slot_rows, flat_in, preferred_element_type=jnp.float32).reshape(-1, 2, FF)
        gate_pre = gate_up[:, 0]
        up_pre = gate_up[:, 1]
        gate_sig = jax.nn.sigmoid(gate_pre)
        hidden = (gate_pre * gate_sig * up_pre).astype(jnp.bfloat16)
        expert_out = jnp.dot(hidden, weight_out, preferred_element_type=jnp.float32).astype(jnp.bfloat16)
        out_total = out_total.at[token_ids].add(slot_weights[:, None] * expert_out.astype(jnp.float32))
        out_grad = (slot_weights[:, None] * cot_table[token_ids].astype(jnp.float32)).astype(jnp.bfloat16)
        hidden_grad = jnp.dot(out_grad, weight_out.T, preferred_element_type=jnp.float32)
        gate_grad = hidden_grad * up_pre * gate_sig * (1.0 + gate_pre * (1.0 - gate_sig))
        up_grad = hidden_grad * gate_pre * gate_sig
        pre_grad = jnp.stack([gate_grad, up_grad], axis=1).astype(jnp.bfloat16).reshape(-1, 2 * FF)
        in_grad = jnp.dot(pre_grad, flat_in.T, preferred_element_type=jnp.float32).astype(jnp.bfloat16)
        grad_total = grad_total.at[token_ids].add(in_grad.astype(jnp.float32))
        grad_in = jnp.dot(slot_rows.T, pre_grad, preferred_element_type=jnp.float32)
        grad_out = jnp.dot(hidden.T, out_grad, preferred_element_type=jnp.float32)
        new_in = came_step(grad_in, flat_in, moment_in.reshape(D, 2 * FF), rows_in, cols_in.reshape(2, 2 * FF))
        new_out = came_step(grad_out, weight_out, moment_out, rows_out, cols_out)
        return ((out_total, grad_total), (new_in[0].reshape(D, 2, FF), new_in[1].reshape(D, 2, FF), new_in[2], new_in[3].reshape(2, 2, FF), new_out[0], new_out[1], new_out[2], new_out[3]))
    start_totals = (jnp.zeros((TOKENS + 1, D), jnp.float32), jnp.zeros((TOKENS + 1, D), jnp.float32))
    final_totals, new_state = lax.scan(expert_step, start_totals, (w_in, w_out, mom_in, mom_out, in_rows, in_cols, out_rows, out_cols, slot_token, slot_gate))
    output = final_totals[0][:TOKENS].astype(jnp.bfloat16)
    grad_tokens = final_totals[1][:TOKENS].astype(jnp.bfloat16)
    return (output, grad_tokens, new_state[0], new_state[4], new_state[1], new_state[5], new_state[2], new_state[3], new_state[6], new_state[7])
```

```python
import functools

import jax
import jax.numpy as jnp
from jax import lax
from jax.experimental import pallas as pl
from jax.experimental.pallas import tpu as pltpu
from jax.sharding import PartitionSpec as P

BETA_ONE = 0.9
BETA_TWO = 0.999
BETA_THREE = 0.9999
EPS_ONE = 1e-30
EPS_TWO = 1e-16
CLIP_LIMIT = 1.0
LEARN_RATE = 0.01
LANES = 128


F32 = jnp.float32
BF16 = jnp.bfloat16
SMEM = pl.BlockSpec(memory_space=pltpu.SMEM)


def pairing(count, step):
    if count & (count - 1) == 0:
        return lambda i: i ^ step, lambda i: i ^ step
    return lambda i: (i + step) % count, lambda i: (i - step) % count


def swap(value, axis, count, step):
    target, _ = pairing(count, step)
    return lax.ppermute(value, axis, [(i, target(i)) for i in range(count)])


def shape(dims, kind):
    return jax.ShapeDtypeStruct(dims, kind)


def dot_nt(a, b):
    return lax.dot_general(a, b, (((1,), (1,)), ((), ())), preferred_element_type=F32)


def dot_tn(a, b):
    return lax.dot_general(a, b, (((0,), (0,)), ((), ())), preferred_element_type=F32)


def prep_kernel(capacity, ids_ref, logits_ref, plan_ref, cot_ref, out_ref):
    choices, tok_rows = ids_ref.shape
    experts = plan_ref.shape[0]
    feat = cot_ref.shape[1]
    lanes = out_ref.shape[1] - feat
    out_ref[:, :feat] = cot_ref[...]
    sig = jax.nn.sigmoid(logits_ref[...])
    gates = sig / jnp.sum(sig, axis=0, keepdims=True)
    expert = lax.broadcasted_iota(jnp.int32, (experts, tok_rows), 0)
    present = jnp.zeros((experts, tok_rows), F32)
    weight = jnp.zeros((experts, tok_rows), F32)
    for k in range(choices):
        hit = ids_ref[k : k + 1, :] == expert
        present = present + jnp.where(hit, 1.0, 0.0)
        weight = weight + jnp.where(hit, gates[k : k + 1, :], 0.0)
    first = lax.broadcasted_iota(jnp.int32, (tok_rows, tok_rows), 0)
    second = lax.broadcasted_iota(jnp.int32, (tok_rows, tok_rows), 1)
    before = jnp.where(first < second, 1.0, 0.0).astype(BF16)
    rank = jnp.dot(present.astype(BF16), before, preferred_element_type=F32)
    limit = jnp.where(plan_ref[...] > 0, 2.0 * capacity, 1.0 * capacity)
    weight = jnp.where((present > 0) & (rank < limit), weight, 0.0)
    high = weight.astype(BF16)
    rest = weight - high.astype(F32)
    middle = rest.astype(BF16)
    low = (rest - middle.astype(F32)).astype(BF16)
    stack = jnp.concatenate(
        [high.astype(F32), middle.astype(F32), low.astype(F32)]
        + ([jnp.zeros((lanes - 3 * experts, tok_rows), F32)] if lanes > 3 * experts else []),
        axis=0,
    )
    same = jnp.where(first == second, 1.0, 0.0).astype(BF16)
    out_ref[:, feat:] = dot_nt(same, stack.astype(BF16)).astype(BF16)


def forward_kernel(pieces, blocks, where_ref, *refs):
    rows_in, w_ref = refs[:pieces], refs[pieces]
    rows_ref, own_ref = refs[pieces + 1 : pieces + 3]
    sends, part_ref = refs[pieces + 3 : -1], refs[-1]
    tok_rows = rows_in[0].shape[0]
    block = own_ref.shape[0]
    for k, ref in enumerate(rows_in):
        rows_ref[k * tok_rows : (k + 1) * tok_rows, :] = ref[...]
    part_ref[...] = jnp.dot(rows_ref[...], w_ref[...], preferred_element_type=F32)
    for d in range(blocks):
        start = pl.multiple_of(where_ref[1 + d] * block, block)
        piece = part_ref[pl.ds(start, block), :]
        if d == 0:
            own_ref[...] = piece
        else:
            sends[d - 1][...] = piece.astype(BF16)


def backward_kernel(pieces, blocks, experts, where_ref, *refs):
    packed, w_ref = refs[:pieces], refs[pieces]
    rows_ref, gate_ref, own_ref = refs[pieces + 1 : pieces + 4]
    sends, part_ref = refs[pieces + 4 : -1], refs[-1]
    tok_rows = packed[0].shape[0]
    feat = rows_ref.shape[1]
    block = own_ref.shape[0]
    lanes = packed[0].shape[1] - feat
    lane = lax.broadcasted_iota(jnp.int32, (tok_rows, lanes), 1)
    me = where_ref[0]
    mine = (lane == me) | (lane == me + experts) | (lane == me + 2 * experts)
    for k, ref in enumerate(packed):
        rows = slice(k * tok_rows, (k + 1) * tok_rows)
        parts = ref[:, feat:].astype(F32)
        gate = jnp.sum(jnp.where(mine, parts, 0.0), axis=1, keepdims=True)
        gate_ref[rows, :] = jnp.broadcast_to(gate, (tok_rows, LANES))
        rows_ref[rows, :] = (ref[:, :feat].astype(F32) * gate).astype(BF16)
    part_ref[...] = dot_nt(rows_ref[...], w_ref[...])
    for d in range(blocks):
        start = pl.multiple_of(where_ref[1 + d] * block, block)
        piece = part_ref[pl.ds(start, block), :]
        if d == 0:
            own_ref[...] = piece
        else:
            sends[d - 1][...] = piece.astype(BF16)


def middle_kernel(blocks, *refs):
    pre, grad, out_ref = refs[:blocks], refs[blocks : 2 * blocks], refs[-1]
    ff = grad[0].shape[1]
    rows = grad[0].shape[0]
    step = 16

    def body(i, carry):
        at = pl.ds(pl.multiple_of(i * step, step), step)

        def total(parts, cols):
            value = parts[0][at, cols]
            for part in parts[1:]:
                value = value + part[at, cols].astype(F32)
            return value

        v = total(pre, slice(0, ff))
        w = total(pre, slice(ff, 2 * ff))
        g = total(grad, slice(0, ff))
        s = jax.nn.sigmoid(v)
        vs = v * s
        out_ref[at, 0:ff] = (vs * w).astype(BF16)
        out_ref[at, ff : 2 * ff] = (g * w * s * (1.0 + v * (1.0 - s))).astype(BF16)
        out_ref[at, 2 * ff : 3 * ff] = (g * vs).astype(BF16)
        return carry

    lax.fori_loop(0, rows // step, body, 0)


def output_kernel(blocks, cores, where_ref, gate_ref, w_in_ref, w_out_ref, *refs):
    pieces = refs[:blocks]
    whole_ref, own_ref = refs[blocks : blocks + 2]
    ff = w_out_ref.shape[0]
    feat = w_out_ref.shape[1]
    block = pieces[0].shape[0]
    half = own_ref.shape[0]
    for d in range(blocks):
        start = pl.multiple_of(where_ref[1 + blocks + d] * block, block)
        whole_ref[pl.ds(start, block), :] = pieces[d][...]
    hidden = whole_ref[:, :ff]
    pre_grad = whole_ref[:, ff:]
    made = jnp.dot(hidden, w_out_ref[...], preferred_element_type=F32)
    made = made * gate_ref[:, :1]
    back = dot_nt(pre_grad, w_in_ref[...])
    own_ref[:, :feat] = made[:half]
    own_ref[:, feat:] = back[:half]
    if cores == 2:
        send_ref = refs[blocks + 2]
        send_ref[:, :feat] = made[half:]
        send_ref[:, feat:] = back[half:]


def pair_kernel(chips, own_ref, got_ref, *outs):
    tok_rows = outs[0].shape[0]
    for d in range(chips):
        rows = slice(d * tok_rows, (d + 1) * tok_rows)
        outs[d][...] = (own_ref[rows, :] + got_ref[rows, :]).astype(outs[d].dtype)


def final_kernel(chips, *refs):
    parts, out_ref, grad_ref = refs[:chips], refs[chips], refs[chips + 1]
    feat = out_ref.shape[1]
    for ref, cols in ((out_ref, slice(0, feat)), (grad_ref, slice(feat, 2 * feat))):
        value = parts[0][:, cols]
        for part in parts[1:]:
            value = value + part[:, cols].astype(F32)
        ref[...] = value.astype(BF16)


def fold(value):
    rows, cols = value.shape
    return jnp.sum(value.reshape(rows // 8, 8, cols), axis=0)


def stats_kernel(
    rows_ref,
    whole_ref,
    out_grad_ref,
    m_in_ref,
    m_out_ref,
    in_rows_col_ref,
    in_rows_ref,
    out_cols_ref,
    stats_ref,
    row_ref,
    col_ref,
    grad_in,
    grad_out,
    acc_in,
    acc_out,
):
    step = pl.program_id(0)
    ff = whole_ref.shape[1] // 3
    tile = rows_ref.shape[1]

    @pl.when(step == 0)
    def _():
        acc_in[...] = jnp.zeros_like(acc_in)
        acc_out[...] = jnp.zeros_like(acc_out)

    grad_in[...] = dot_tn(rows_ref[...], whole_ref[:, ff:])
    grad_out[...] = dot_tn(whole_ref[:, :ff], out_grad_ref[...])
    chunk = 16

    def in_body(i, carry):
        at = pl.ds(pl.multiple_of(i * chunk, chunk), chunk)
        g = grad_in[at, :]
        m = m_in_ref[at, :].astype(F32)
        sq = g * g
        mean = jnp.sum(sq, axis=1, keepdims=True) / (2 * ff)
        row_v = BETA_TWO * in_rows_col_ref[at, 0:1] + (1.0 - BETA_TWO) * (mean + EPS_ONE)
        scale = lax.rsqrt(row_v)
        row_ref[at, 0:1] = row_v
        row_ref[at, 1:2] = scale
        h = g * scale
        acc_in[0] += fold(sq)
        acc_in[1] += fold(h * h)
        acc_in[2] += fold(h * m)
        acc_in[3] += fold(m * m)
        return carry

    lax.fori_loop(0, tile // chunk, in_body, 0)
    out_chunk = 32

    def col_body(i, carry):
        at = pl.ds(pl.multiple_of(i * out_chunk, out_chunk), out_chunk)
        g = grad_out[at, :]
        return carry + fold(g * g)

    col_sq = lax.fori_loop(0, ff // out_chunk, col_body, jnp.zeros((8, tile), F32))
    col_v = BETA_TWO * out_cols_ref[0:1, :] + (1.0 - BETA_TWO) * (
        jnp.sum(col_sq, axis=0, keepdims=True) / ff + EPS_ONE
    )
    col_ref[...] = jnp.broadcast_to(col_v, col_ref.shape)
    col_scale = lax.rsqrt(col_v)

    def squeeze(value):
        total = value[:, :LANES]
        for k in range(1, tile // LANES):
            total = total + value[:, k * LANES : (k + 1) * LANES]
        return total

    def out_body(i, carry):
        at = pl.ds(pl.multiple_of(i * out_chunk, out_chunk), out_chunk)
        g = grad_out[at, :]
        m = m_out_ref[at, :].astype(F32)
        h = g * col_scale
        acc_out[0, at, :] += squeeze(g * g)
        acc_out[1, at, :] += squeeze(h * h)
        acc_out[2, at, :] += squeeze(h * m)
        acc_out[3, at, :] += squeeze(m * m)
        return carry

    lax.fori_loop(0, ff // out_chunk, out_body, 0)

    @pl.when(step == pl.num_programs(0) - 1)
    def _():
        stats_ref[...] = jnp.zeros_like(stats_ref)
        for k in range(4):
            stats_ref[k : k + 1, : 2 * ff] = jnp.sum(acc_in[k], axis=0, keepdims=True)
            stats_ref[k : k + 1, 2 * ff :] = jnp.sum(
                jnp.transpose(acc_out[k]), axis=0, keepdims=True
            )
        for k in range(2):
            total = jnp.sum(in_rows_ref[k : k + 1, :], axis=1, keepdims=True)
            stats_ref[4 + k : 5 + k, :LANES] = jnp.broadcast_to(total, (1, LANES))


def update_kernel(
    full_rows,
    rows_ref,
    whole_ref,
    out_grad_ref,
    m_in_ref,
    m_out_ref,
    w_in_ref,
    w_out_ref,
    in_rows_col_ref,
    in_cols_ref,
    out_rows_ref,
    out_cols_ref,
    row_ref,
    col_ref,
    *refs,
):
    stats = refs[:-12]
    (
        new_w_in_ref,
        new_w_out_ref,
        new_m_in_ref,
        new_m_out_ref,
        new_in_rows_ref,
        new_in_cols_ref,
        new_out_rows_ref,
        new_out_cols_ref,
        grad_in,
        grad_out,
        lane_in,
        sub_out,
    ) = refs[-12:]
    ff = whole_ref.shape[1] // 3
    tile = rows_ref.shape[1]
    keep = BETA_ONE * BETA_ONE

    @pl.when(pl.program_id(0) == 0)
    def _():
        total = stats[0][...]
        for ref in stats[1:]:
            total = total + ref[...]
        col_sq, col_s, col_x, col_n = (total[k : k + 1, : 2 * ff] for k in range(4))
        row_sq, row_s, row_x, row_n = (total[k : k + 1, 2 * ff :] for k in range(4))
        sum_v = total[4:5, 0:1]
        sum_r = total[5:6, 0:1]
        count = full_rows * 2 * ff

        def over(value):
            return jnp.sum(value, axis=1, keepdims=True)

        col_v = BETA_TWO * in_cols_ref[0:1, :] + (1.0 - BETA_TWO) * (
            col_sq / full_rows + EPS_ONE
        )
        row_v = BETA_TWO * out_rows_ref[0:1, :] + (1.0 - BETA_TWO) * (
            row_sq / full_rows + EPS_ONE
        )
        mean_v_in = BETA_TWO * sum_v / full_rows + (1.0 - BETA_TWO) * (
            over(col_sq) / count + EPS_ONE
        )
        mean_v_out = over(row_v) / ff
        norm_in = mean_v_in * over(col_s / col_v) / count
        norm_out = mean_v_out * over(row_s / row_v) / (ff * full_rows)
        cb = (
            lax.rsqrt(col_v)
            * jnp.sqrt(mean_v_in)
            / jnp.maximum(1.0, jnp.sqrt(norm_in) / CLIP_LIMIT)
        )
        ra = (
            lax.rsqrt(row_v)
            * jnp.sqrt(mean_v_out)
            / jnp.maximum(1.0, jnp.sqrt(norm_out) / CLIP_LIMIT)
        )
        res_col = keep * (cb * (cb * col_s - 2.0 * col_x) + col_n)
        res_row = keep * (ra * (ra * row_s - 2.0 * row_x) + row_n)
        col_r = BETA_THREE * in_cols_ref[1:2, :] + (1.0 - BETA_THREE) * (
            res_col / full_rows + EPS_TWO
        )
        row_r = BETA_THREE * out_rows_ref[1:2, :] + (1.0 - BETA_THREE) * (
            res_row / full_rows + EPS_TWO
        )
        mean_r_in = BETA_THREE * sum_r / full_rows + (1.0 - BETA_THREE) * (
            over(res_col) / count + EPS_TWO
        )
        mean_r_out = over(row_r) / ff
        lane_in[0:1, :] = cb
        lane_in[1:2, :] = LEARN_RATE * jnp.sqrt(mean_r_in) * lax.rsqrt(col_r)
        step_row = LEARN_RATE * jnp.sqrt(mean_r_out) * lax.rsqrt(row_r)
        sub = lax.broadcasted_iota(jnp.int32, (LANES, ff), 0)
        sub_out[...] = jnp.transpose(jnp.where(sub == 0, ra, step_row))
        for k in range(2):
            new_in_cols_ref[0, k : k + 1, :] = col_v[:, k * ff : (k + 1) * ff]
            new_in_cols_ref[1, k : k + 1, :] = col_r[:, k * ff : (k + 1) * ff]
        new_out_rows_ref[0:1, :] = row_v
        new_out_rows_ref[1:2, :] = row_r

    grad_in[...] = dot_tn(rows_ref[...], whole_ref[:, ff:])
    grad_out[...] = dot_tn(whole_ref[:, :ff], out_grad_ref[...])
    chunk = 16
    groups = tile // LANES
    for group in range(groups):
        lane = lax.broadcasted_iota(jnp.int32, (chunk, LANES), 1)
        pieces = []
        for i in range(LANES // chunk):
            first = group * LANES + i * chunk
            at = slice(first, first + chunk)
            m = m_in_ref[at, :].astype(F32)
            u = grad_in[at, :] * row_ref[at, 1:2] * lane_in[0:1, :]
            diff = u - m
            mean = jnp.sum(diff * diff, axis=1, keepdims=True) * (keep / (2 * ff))
            row_r = BETA_THREE * in_rows_col_ref[at, 1:2] + (1.0 - BETA_THREE) * (
                mean + EPS_TWO
            )
            moment = BETA_ONE * m + (1.0 - BETA_ONE) * u
            new_w = w_in_ref[at, :].astype(F32) - moment * lax.rsqrt(row_r) * lane_in[1:2, :]
            for k in range(2):
                cols = slice(k * ff, (k + 1) * ff)
                new_m_in_ref[at, k, :] = moment[:, cols].astype(BF16)
                new_w_in_ref[at, k, :] = new_w[:, cols].astype(BF16)
            pieces.append(jnp.where(lane == 0, row_ref[at, 0:1], row_r))
        turned = jnp.transpose(jnp.concatenate(pieces, axis=0))
        new_in_rows_ref[:, group * LANES : (group + 1) * LANES] = turned[0:2, :]

    out_chunk = 32
    col_v = col_ref[0:1, :]
    col_scale = lax.rsqrt(col_v)

    def res_body(i, carry):
        at = pl.ds(pl.multiple_of(i * out_chunk, out_chunk), out_chunk)
        m = m_out_ref[at, :].astype(F32)
        diff = grad_out[at, :] * sub_out[at, 0:1] * col_scale - m
        return carry + fold(diff * diff)

    res = lax.fori_loop(0, ff // out_chunk, res_body, jnp.zeros((8, tile), F32))
    col_r = BETA_THREE * out_cols_ref[1:2, :] + (1.0 - BETA_THREE) * (
        jnp.sum(res, axis=0, keepdims=True) * (keep / ff) + EPS_TWO
    )
    col_step = lax.rsqrt(col_r)

    def out_body(i, carry):
        at = pl.ds(pl.multiple_of(i * out_chunk, out_chunk), out_chunk)
        m = m_out_ref[at, :].astype(F32)
        u = grad_out[at, :] * sub_out[at, 0:1] * col_scale
        moment = BETA_ONE * m + (1.0 - BETA_ONE) * u
        new_m_out_ref[at, :] = moment.astype(BF16)
        new_w_out_ref[at, :] = (
            w_out_ref[at, :].astype(F32) - moment * sub_out[at, 1:2] * col_step
        ).astype(BF16)
        return carry

    lax.fori_loop(0, ff // out_chunk, out_body, 0)
    new_out_cols_ref[0:1, :] = col_v
    new_out_cols_ref[1:2, :] = col_r


def per_device(
    tokens,
    cotangent,
    expert_ids,
    gate_logits,
    shadow_plan,
    w_in,
    w_out,
    mom_in,
    mom_out,
    in_rows,
    in_cols,
    out_rows,
    out_cols,
):
    groups = lax.axis_size("expert")
    fsdp_count = lax.axis_size("fsdp")
    fsdp_id = lax.axis_index("fsdp")
    tok_rows, topk_width = expert_ids.shape
    experts = shadow_plan.shape[0]
    feat = tokens.shape[1]
    ff = w_in.shape[3]
    full_rows = feat * fsdp_count
    capacity = tok_rows * topk_width // groups
    cores = 2 if groups % 2 == 0 else 1
    chips = groups // cores
    all_rows = groups * tok_rows
    half = all_rows // cores
    block = all_rows // fsdp_count
    w_in2 = w_in[0].reshape(feat, 2 * ff)
    m_in2 = mom_in[0].reshape(feat, 2 * ff)
    w_out2 = w_out[0]
    m_out2 = mom_out[0]
    lanes = -(-3 * experts // LANES) * LANES
    where = jnp.stack(
        [lax.axis_index("expert")]
        + [pairing(fsdp_count, d)[0](fsdp_id) for d in range(fsdp_count)]
        + [pairing(fsdp_count, d)[1](fsdp_id) for d in range(fsdp_count)]
    ).astype(jnp.int32)
    params = pltpu.CompilerParams(vmem_limit_bytes=48 * 1024 * 1024)

    packed = pl.pallas_call(
        functools.partial(prep_kernel, capacity),
        out_shape=shape((tok_rows, feat + lanes), BF16),
        name="prep",
    )(expert_ids.T, gate_logits.T, shadow_plan.reshape(experts, 1), cotangent)

    def gather_expert(value):
        pieces = [value] + [swap(value, "expert", groups, cores * d) for d in range(1, chips)]
        others = [swap(p, "expert", groups, 1) for p in pieces] if cores == 2 else []
        return pieces + others

    def whole_specs(count):
        return [pl.BlockSpec(memory_space=pltpu.VMEM)] * count

    token_pieces = gather_expert(tokens)
    rows_x, *pre = pl.pallas_call(
        functools.partial(forward_kernel, groups, fsdp_count),
        in_specs=[SMEM] + whole_specs(groups + 1),
        out_shape=[shape((all_rows, feat), BF16), shape((block, 2 * ff), F32)]
        + [shape((block, 2 * ff), BF16)] * (fsdp_count - 1),
        scratch_shapes=[pltpu.VMEM((all_rows, 2 * ff), F32)],
        compiler_params=params,
        name="forward",
    )(where, *token_pieces, w_in2)
    pre = [pre[0]] + [swap(pre[d], "fsdp", fsdp_count, d) for d in range(1, fsdp_count)]

    packed_pieces = gather_expert(packed)
    rows_o, gate, *hid = pl.pallas_call(
        functools.partial(backward_kernel, groups, fsdp_count, experts),
        in_specs=[SMEM] + whole_specs(groups + 1),
        out_shape=[
            shape((all_rows, feat), BF16),
            shape((all_rows, LANES), F32),
            shape((block, ff), F32),
        ]
        + [shape((block, ff), BF16)] * (fsdp_count - 1),
        scratch_shapes=[pltpu.VMEM((all_rows, ff), F32)],
        compiler_params=params,
        name="backward",
    )(where, *packed_pieces, w_out2)
    hid = [hid[0]] + [swap(hid[d], "fsdp", fsdp_count, d) for d in range(1, fsdp_count)]

    made = pl.pallas_call(
        functools.partial(middle_kernel, fsdp_count),
        out_shape=shape((block, 3 * ff), BF16),
        compiler_params=params,
        name="middle",
    )(*pre, *hid)
    made = [made] + [swap(made, "fsdp", fsdp_count, d) for d in range(1, fsdp_count)]

    whole, *back = pl.pallas_call(
        functools.partial(output_kernel, fsdp_count, cores),
        in_specs=[SMEM] + whole_specs(3 + fsdp_count),
        out_shape=[shape((all_rows, 3 * ff), BF16)]
        + [shape((half, 2 * feat), F32)] * cores,
        compiler_params=params,
        name="outputs",
    )(where, gate, w_in2, w_out2, *made)
    if cores == 2:
        got = swap(back[1], "expert", groups, 1)
        sums = pl.pallas_call(
            functools.partial(pair_kernel, chips),
            out_shape=[shape((tok_rows, 2 * feat), F32)]
            + [shape((tok_rows, 2 * feat), BF16)] * (chips - 1),
            compiler_params=params,
            name="pair",
        )(back[0], got)
    else:
        sums = [back[0][d * tok_rows : (d + 1) * tok_rows] for d in range(chips)]
    sums = [sums[0]] + [swap(sums[d], "expert", groups, cores * d) for d in range(1, chips)]
    output, grad_tokens = pl.pallas_call(
        functools.partial(final_kernel, chips),
        out_shape=[shape((tok_rows, feat), BF16)] * 2,
        compiler_params=params,
        name="final",
    )(*sums)

    tile = min(feat, 256)
    steps = feat // tile
    col_tile = lambda rows: pl.BlockSpec((rows, tile), lambda i: (0, i))
    row_tile = lambda cols: pl.BlockSpec((tile, cols), lambda i: (i, 0))
    full = lambda *dims: pl.BlockSpec(dims, lambda i: (0,) * len(dims))
    in_rows_col = in_rows[0].T
    in_cols2 = in_cols[0].reshape(2, 2 * ff)
    stats, row_state, col_state = pl.pallas_call(
        stats_kernel,
        grid=(steps,),
        in_specs=[
            col_tile(all_rows),
            full(all_rows, 3 * ff),
            col_tile(all_rows),
            row_tile(2 * ff),
            col_tile(ff),
            row_tile(2),
            full(2, feat),
            col_tile(2),
        ],
        out_specs=[full(8, 3 * ff), row_tile(2), col_tile(8)],
        out_shape=[shape((8, 3 * ff), F32), shape((feat, 2), F32), shape((8, feat), F32)],
        scratch_shapes=[
            pltpu.VMEM((tile, 2 * ff), F32),
            pltpu.VMEM((ff, tile), F32),
            pltpu.VMEM((4, 8, 2 * ff), F32),
            pltpu.VMEM((4, ff, LANES), F32),
        ],
        compiler_params=params,
        name="stats",
    )(rows_x, whole, rows_o, m_in2, m_out2, in_rows_col, in_rows[0], out_cols[0])
    stats = [stats] + [swap(stats, "fsdp", fsdp_count, d) for d in range(1, fsdp_count)]

    new = pl.pallas_call(
        functools.partial(update_kernel, full_rows),
        grid=(steps,),
        in_specs=[
            col_tile(all_rows),
            full(all_rows, 3 * ff),
            col_tile(all_rows),
            row_tile(2 * ff),
            col_tile(ff),
            row_tile(2 * ff),
            col_tile(ff),
            row_tile(2),
            full(2, 2 * ff),
            full(2, ff),
            col_tile(2),
            row_tile(2),
            col_tile(8),
        ]
        + [full(8, 3 * ff)] * fsdp_count,
        out_specs=[
            pl.BlockSpec((tile, 2, ff), lambda i: (i, 0, 0)),
            col_tile(ff),
            pl.BlockSpec((tile, 2, ff), lambda i: (i, 0, 0)),
            col_tile(ff),
            col_tile(2),
            full(2, 2, ff),
            full(2, ff),
            col_tile(2),
        ],
        out_shape=[
            shape((feat, 2, ff), BF16),
            shape((ff, feat), BF16),
            shape((feat, 2, ff), BF16),
            shape((ff, feat), BF16),
            shape((2, feat), F32),
            shape((2, 2, ff), F32),
            shape((2, ff), F32),
            shape((2, feat), F32),
        ],
        scratch_shapes=[
            pltpu.VMEM((tile, 2 * ff), F32),
            pltpu.VMEM((ff, tile), F32),
            pltpu.VMEM((8, 2 * ff), F32),
            pltpu.VMEM((ff, LANES), F32),
        ],
        compiler_params=params,
        name="update",
    )(
        rows_x,
        whole,
        rows_o,
        m_in2,
        m_out2,
        w_in2,
        w_out2,
        in_rows_col,
        in_cols2,
        out_rows[0],
        out_cols[0],
        row_state,
        col_state,
        *stats,
    )
    return (output, grad_tokens, *[value[None] for value in new])


def solution(mesh):
    return jax.shard_map(
        per_device,
        mesh=mesh,
        in_specs=(
            P("expert", "fsdp"),
            P("expert", "fsdp"),
            P("expert", None),
            P("expert", None),
            P(),
            P("expert", "fsdp", None, None),
            P("expert", None, "fsdp"),
            P("expert", "fsdp", None, None),
            P("expert", None, "fsdp"),
            P("expert", None, "fsdp"),
            P("expert", None, None, None),
            P("expert", None, None),
            P("expert", None, "fsdp"),
        ),
        out_specs=(
            P("expert", "fsdp"),
            P("expert", "fsdp"),
            P("expert", "fsdp", None, None),
            P("expert", None, "fsdp"),
            P("expert", "fsdp", None, None),
            P("expert", None, "fsdp"),
            P("expert", None, "fsdp"),
            P("expert", None, None, None),
            P("expert", None, None),
            P("expert", None, "fsdp"),
        ),
        check_vma=False,
    )
```

```python
import functools

import jax
import jax.numpy as jnp
from jax import lax
from jax.experimental import pallas as pl
from jax.experimental.pallas import tpu as pltpu
from jax.sharding import PartitionSpec as P


BETA_ONE = 0.9
BETA_TWO = 0.999
BETA_THREE = 0.9999
EPS_ONE = 1e-30
EPS_TWO = 1e-16
CLIP_LIMIT = 1.0
LEARN_RATE = 0.01
LANES = 128


F32 = jnp.float32
BF16 = jnp.bfloat16
SMEM = pl.BlockSpec(memory_space=pltpu.SMEM)


def pairing(count, step):
    if count & (count - 1) == 0:
        return lambda i: i ^ step, lambda i: i ^ step
    return lambda i: (i + step) % count, lambda i: (i - step) % count


def swap(value, axis, count, step):
    target, _ = pairing(count, step)
    return lax.ppermute(value, axis, [(i, target(i)) for i in range(count)])


def shape(dims, kind):
    return jax.ShapeDtypeStruct(dims, kind)


def dot_nt(a, b):
    return lax.dot_general(a, b, (((1,), (1,)), ((), ())), preferred_element_type=F32)


def dot_tn(a, b):
    return lax.dot_general(a, b, (((0,), (0,)), ((), ())), preferred_element_type=F32)


def prep_kernel(
    capacity, plan_ref, ids_hbm, logits_hbm, cot_hbm, out_hbm, ids_ref, logits_ref, gate_ref, sems
):
    choices, tok_rows = ids_ref.shape
    experts = plan_ref.shape[0]
    feat = cot_hbm.shape[1]
    lanes = gate_ref.shape[1]
    body = pltpu.make_async_copy(cot_hbm, out_hbm.at[:, pl.ds(0, feat)], sems.at[0])
    ids_copy = pltpu.make_async_copy(ids_hbm, ids_ref, sems.at[1])
    logits_copy = pltpu.make_async_copy(logits_hbm, logits_ref, sems.at[2])
    body.start()
    ids_copy.start()
    logits_copy.start()
    ids_copy.wait()
    logits_copy.wait()
    sig = jax.nn.sigmoid(logits_ref[...])
    gates = sig / jnp.sum(sig, axis=0, keepdims=True)
    expert = lax.broadcasted_iota(jnp.int32, (experts, tok_rows), 0)
    present = jnp.zeros((experts, tok_rows), F32)
    weight = jnp.zeros((experts, tok_rows), F32)
    for k in range(choices):
        hit = ids_ref[k : k + 1, :] == expert
        present = present + jnp.where(hit, 1.0, 0.0)
        weight = weight + jnp.where(hit, gates[k : k + 1, :], 0.0)
    first = lax.broadcasted_iota(jnp.int32, (tok_rows, tok_rows), 0)
    second = lax.broadcasted_iota(jnp.int32, (tok_rows, tok_rows), 1)
    before = jnp.where(first < second, 1.0, 0.0).astype(BF16)
    rank = jnp.dot(present.astype(BF16), before, preferred_element_type=F32)
    limit = jnp.zeros((experts, tok_rows), jnp.int32)
    for e in range(experts):
        allowed = jnp.where(plan_ref[e] > 0, 2 * capacity, capacity)
        limit = jnp.where(expert == e, allowed, limit)
    limit = limit.astype(F32)
    weight = jnp.where((present > 0) & (rank < limit), weight, 0.0)
    high = weight.astype(BF16)
    rest = weight - high.astype(F32)
    middle = rest.astype(BF16)
    low = (rest - middle.astype(F32)).astype(BF16)
    stack = jnp.concatenate(
        [high.astype(F32), middle.astype(F32), low.astype(F32)]
        + ([jnp.zeros((lanes - 3 * experts, tok_rows), F32)] if lanes > 3 * experts else []),
        axis=0,
    )
    same = jnp.where(first == second, 1.0, 0.0).astype(BF16)
    gate_ref[...] = dot_nt(same, stack.astype(BF16)).astype(BF16)
    tail = pltpu.make_async_copy(gate_ref, out_hbm.at[:, pl.ds(feat, lanes)], sems.at[3])
    tail.start()
    tail.wait()
    body.wait()


def forward_kernel(pieces, blocks, where_ref, *refs):
    rows_in, w_ref = refs[:pieces], refs[pieces]
    rows_ref, own_ref = refs[pieces + 1 : pieces + 3]
    sends, part_ref = refs[pieces + 3 : -1], refs[-1]
    tok_rows = rows_in[0].shape[0]
    block = own_ref.shape[0]
    for k, ref in enumerate(rows_in):
        rows_ref[k * tok_rows : (k + 1) * tok_rows, :] = ref[...]
    part_ref[...] = jnp.dot(rows_ref[...], w_ref[...], preferred_element_type=F32)
    for d in range(blocks):
        start = pl.multiple_of(where_ref[1 + d] * block, block)
        piece = part_ref[pl.ds(start, block), :]
        if d == 0:
            own_ref[...] = piece
        else:
            sends[d - 1][...] = piece.astype(BF16)


def backward_kernel(pieces, blocks, experts, where_ref, *refs):
    packed, w_ref = refs[:pieces], refs[pieces]
    rows_ref, gate_ref, own_ref = refs[pieces + 1 : pieces + 4]
    sends, part_ref = refs[pieces + 4 : -1], refs[-1]
    tok_rows = packed[0].shape[0]
    feat = rows_ref.shape[1]
    block = own_ref.shape[0]
    lanes = packed[0].shape[1] - feat
    lane = lax.broadcasted_iota(jnp.int32, (tok_rows, lanes), 1)
    me = where_ref[0]
    mine = (lane == me) | (lane == me + experts) | (lane == me + 2 * experts)
    for k, ref in enumerate(packed):
        rows = slice(k * tok_rows, (k + 1) * tok_rows)
        parts = ref[:, feat:].astype(F32)
        gate = jnp.sum(jnp.where(mine, parts, 0.0), axis=1, keepdims=True)
        gate_ref[rows, :] = jnp.broadcast_to(gate, (tok_rows, LANES))
        rows_ref[rows, :] = (ref[:, :feat].astype(F32) * gate).astype(BF16)
    part_ref[...] = dot_nt(rows_ref[...], w_ref[...])
    for d in range(blocks):
        start = pl.multiple_of(where_ref[1 + d] * block, block)
        piece = part_ref[pl.ds(start, block), :]
        if d == 0:
            own_ref[...] = piece
        else:
            sends[d - 1][...] = piece.astype(BF16)


def middle_kernel(blocks, *refs):
    pre, grad, out_ref = refs[:blocks], refs[blocks : 2 * blocks], refs[-1]
    ff = grad[0].shape[1]
    rows = grad[0].shape[0]
    step = 16

    def body(i, carry):
        at = pl.ds(pl.multiple_of(i * step, step), step)

        def total(parts, cols):
            value = parts[0][at, cols]
            for part in parts[1:]:
                value = value + part[at, cols].astype(F32)
            return value

        v = total(pre, slice(0, ff))
        w = total(pre, slice(ff, 2 * ff))
        g = total(grad, slice(0, ff))
        s = jax.nn.sigmoid(v)
        vs = v * s
        out_ref[at, 0:ff] = (vs * w).astype(BF16)
        out_ref[at, ff : 2 * ff] = (g * w * s * (1.0 + v * (1.0 - s))).astype(BF16)
        out_ref[at, 2 * ff : 3 * ff] = (g * vs).astype(BF16)
        return carry

    lax.fori_loop(0, rows // step, body, 0)


def output_kernel(blocks, cores, where_ref, gate_ref, w_in_ref, w_out_ref, *refs):
    pieces = refs[:blocks]
    whole_ref, own_ref = refs[blocks : blocks + 2]
    ff = w_out_ref.shape[0]
    feat = w_out_ref.shape[1]
    block = pieces[0].shape[0]
    half = own_ref.shape[0]
    for d in range(blocks):
        start = pl.multiple_of(where_ref[1 + blocks + d] * block, block)
        whole_ref[pl.ds(start, block), :] = pieces[d][...]
    hidden = whole_ref[:, :ff]
    pre_grad = whole_ref[:, ff:]
    made = jnp.dot(hidden, w_out_ref[...], preferred_element_type=F32)
    made = made * gate_ref[:, :1]
    back = dot_nt(pre_grad, w_in_ref[...])
    own_ref[:, :feat] = made[:half]
    own_ref[:, feat:] = back[:half]
    if cores == 2:
        send_ref = refs[blocks + 2]
        send_ref[:, :feat] = made[half:]
        send_ref[:, feat:] = back[half:]


def pair_kernel(chips, own_ref, got_ref, *outs):
    tok_rows = outs[0].shape[0]
    for d in range(chips):
        rows = slice(d * tok_rows, (d + 1) * tok_rows)
        outs[d][...] = (own_ref[rows, :] + got_ref[rows, :]).astype(outs[d].dtype)


def final_kernel(chips, *refs):
    parts, out_ref, grad_ref = refs[:chips], refs[chips], refs[chips + 1]
    feat = out_ref.shape[1]
    for ref, cols in ((out_ref, slice(0, feat)), (grad_ref, slice(feat, 2 * feat))):
        value = parts[0][:, cols]
        for part in parts[1:]:
            value = value + part[:, cols].astype(F32)
        ref[...] = value.astype(BF16)


def fold(value):
    rows, cols = value.shape
    return jnp.sum(value.reshape(rows // 8, 8, cols), axis=0)


def turned(row):
    return jnp.transpose(jnp.broadcast_to(row, (LANES, row.shape[1])))


def stats_kernel(
    rows_ref,
    whole_ref,
    out_grad_ref,
    m_in_ref,
    m_out_ref,
    in_rows_ref,
    out_cols_ref,
    stats_ref,
    row_ref,
    col_ref,
    grad_in,
    grad_out,
    acc_in,
    acc_out,
):
    step = pl.program_id(0)
    ff = whole_ref.shape[1] // 3
    tile = rows_ref.shape[1]

    @pl.when(step == 0)
    def _():
        acc_in[...] = jnp.zeros_like(acc_in)
        acc_out[...] = jnp.zeros_like(acc_out)

    grad_in[...] = dot_tn(rows_ref[...], whole_ref[:, ff:])
    grad_out[...] = dot_tn(whole_ref[:, :ff], out_grad_ref[...])
    chunk = 16

    def row_body(i, carry):
        at = pl.ds(pl.multiple_of(i * chunk, chunk), chunk)
        g = grad_in[at, :]
        row_ref[at, 0:1] = jnp.sum(g * g, axis=1, keepdims=True)
        return carry

    lax.fori_loop(0, tile // chunk, row_body, 0, unroll=4)
    mean = row_ref[:, 0:1] / (2 * ff)
    span = pl.ds(pl.multiple_of(step * tile, tile), tile)
    old = turned(in_rows_ref[0, 0:1, span])
    row_v = BETA_TWO * old[:, 0:1] + (1.0 - BETA_TWO) * (mean + EPS_ONE)
    row_ref[:, 0:1] = row_v
    row_ref[:, 1:2] = lax.rsqrt(row_v)
    slab = 4 * LANES
    for first in range(0, 2 * ff, slab):
        cols = slice(first, min(first + slab, 2 * ff))

        def in_body(i, carry):
            at = pl.ds(pl.multiple_of(i * chunk, chunk), chunk)
            g = grad_in[at, cols]
            m = m_in_ref[at, cols].astype(F32)
            h = g * row_ref[at, 1:2]
            parts = (g * g, h * h, h * m, m * m)
            return tuple(c + fold(p) for c, p in zip(carry, parts))

        zero = jnp.zeros((8, cols.stop - cols.start), F32)
        sums = lax.fori_loop(0, tile // chunk, in_body, (zero,) * 4, unroll=4)
        for k in range(4):
            acc_in[k, :, cols] += sums[k]
    out_chunk = 32

    def col_body(i, carry):
        at = pl.ds(pl.multiple_of(i * out_chunk, out_chunk), out_chunk)
        g = grad_out[at, :]
        return carry + fold(g * g)

    col_sq = lax.fori_loop(
        0, ff // out_chunk, col_body, jnp.zeros((8, tile), F32), unroll=4
    )
    col_v = BETA_TWO * out_cols_ref[0, 0:1, :] + (1.0 - BETA_TWO) * (
        jnp.sum(col_sq, axis=0, keepdims=True) / ff + EPS_ONE
    )
    col_ref[...] = jnp.broadcast_to(col_v, col_ref.shape)
    col_scale = lax.rsqrt(col_v)

    def squeeze(value):
        total = value[:, :LANES]
        for k in range(1, tile // LANES):
            total = total + value[:, k * LANES : (k + 1) * LANES]
        return total

    def out_body(i, carry):
        at = pl.ds(pl.multiple_of(i * out_chunk, out_chunk), out_chunk)
        g = grad_out[at, :]
        m = m_out_ref[at, :].astype(F32)
        h = g * col_scale
        acc_out[0, at, :] += squeeze(g * g)
        acc_out[1, at, :] += squeeze(h * h)
        acc_out[2, at, :] += squeeze(h * m)
        acc_out[3, at, :] += squeeze(m * m)
        return carry

    lax.fori_loop(0, ff // out_chunk, out_body, 0, unroll=4)

    @pl.when(step == pl.num_programs(0) - 1)
    def _():
        stats_ref[...] = jnp.zeros_like(stats_ref)
        for k in range(4):
            stats_ref[k : k + 1, : 2 * ff] = jnp.sum(acc_in[k], axis=0, keepdims=True)
            stats_ref[k : k + 1, 2 * ff :] = jnp.sum(
                jnp.transpose(acc_out[k]), axis=0, keepdims=True
            )
        for k in range(2):
            total = jnp.sum(in_rows_ref[0, k : k + 1, :], axis=1, keepdims=True)
            stats_ref[4 + k : 5 + k, :LANES] = jnp.broadcast_to(total, (1, LANES))


def update_kernel(
    full_rows,
    rows_ref,
    whole_ref,
    out_grad_ref,
    m_in_ref,
    m_out_ref,
    w_in_ref,
    w_out_ref,
    in_rows_ref,
    in_cols_ref,
    out_rows_ref,
    out_cols_ref,
    row_ref,
    col_ref,
    *refs,
):
    stats = refs[:-12]
    (
        new_w_in_ref,
        new_w_out_ref,
        new_m_in_ref,
        new_m_out_ref,
        new_in_rows_ref,
        new_in_cols_ref,
        new_out_rows_ref,
        new_out_cols_ref,
        grad_in,
        grad_out,
        lane_in,
        sub_out,
    ) = refs[-12:]
    ff = whole_ref.shape[1] // 3
    tile = rows_ref.shape[1]
    keep = BETA_ONE * BETA_ONE

    @pl.when(pl.program_id(0) == 0)
    def _():
        total = stats[0][...]
        for ref in stats[1:]:
            total = total + ref[...]
        col_sq, col_s, col_x, col_n = (total[k : k + 1, : 2 * ff] for k in range(4))
        row_sq, row_s, row_x, row_n = (total[k : k + 1, 2 * ff :] for k in range(4))
        sum_v = total[4:5, 0:1]
        sum_r = total[5:6, 0:1]
        count = full_rows * 2 * ff

        def over(value):
            return jnp.sum(value, axis=1, keepdims=True)

        def old_cols(which):
            return jnp.concatenate([in_cols_ref[0, which, k : k + 1, :] for k in range(2)], axis=1)

        col_v = BETA_TWO * old_cols(0) + (1.0 - BETA_TWO) * (
            col_sq / full_rows + EPS_ONE
        )
        row_v = BETA_TWO * out_rows_ref[0, 0:1, :] + (1.0 - BETA_TWO) * (
            row_sq / full_rows + EPS_ONE
        )
        mean_v_in = BETA_TWO * sum_v / full_rows + (1.0 - BETA_TWO) * (
            over(col_sq) / count + EPS_ONE
        )
        mean_v_out = over(row_v) / ff
        norm_in = mean_v_in * over(col_s / col_v) / count
        norm_out = mean_v_out * over(row_s / row_v) / (ff * full_rows)
        cb = (
            lax.rsqrt(col_v)
            * jnp.sqrt(mean_v_in)
            / jnp.maximum(1.0, jnp.sqrt(norm_in) / CLIP_LIMIT)
        )
        ra = (
            lax.rsqrt(row_v)
            * jnp.sqrt(mean_v_out)
            / jnp.maximum(1.0, jnp.sqrt(norm_out) / CLIP_LIMIT)
        )
        res_col = keep * (cb * (cb * col_s - 2.0 * col_x) + col_n)
        res_row = keep * (ra * (ra * row_s - 2.0 * row_x) + row_n)
        col_r = BETA_THREE * old_cols(1) + (1.0 - BETA_THREE) * (
            res_col / full_rows + EPS_TWO
        )
        row_r = BETA_THREE * out_rows_ref[0, 1:2, :] + (1.0 - BETA_THREE) * (
            res_row / full_rows + EPS_TWO
        )
        mean_r_in = BETA_THREE * sum_r / full_rows + (1.0 - BETA_THREE) * (
            over(res_col) / count + EPS_TWO
        )
        mean_r_out = over(row_r) / ff
        lane_in[0:1, :] = cb
        lane_in[1:2, :] = LEARN_RATE * jnp.sqrt(mean_r_in) * lax.rsqrt(col_r)
        step_row = LEARN_RATE * jnp.sqrt(mean_r_out) * lax.rsqrt(row_r)
        sub_out[0] = turned(ra)
        sub_out[1] = turned(step_row)
        for k in range(2):
            new_in_cols_ref[0, k : k + 1, :] = col_v[:, k * ff : (k + 1) * ff]
            new_in_cols_ref[1, k : k + 1, :] = col_r[:, k * ff : (k + 1) * ff]
        new_out_rows_ref[0:1, :] = row_v
        new_out_rows_ref[1:2, :] = row_r

    grad_in[...] = dot_tn(rows_ref[...], whole_ref[:, ff:])
    grad_out[...] = dot_tn(whole_ref[:, :ff], out_grad_ref[...])
    chunk = 16
    groups = tile // LANES
    for group in range(groups):
        lane = lax.broadcasted_iota(jnp.int32, (chunk, LANES), 1)
        pieces = []
        old = turned(in_rows_ref[0, 1:2, group * LANES : (group + 1) * LANES])
        for i in range(LANES // chunk):
            first = group * LANES + i * chunk
            at = slice(first, first + chunk)
            m = m_in_ref[at, :].astype(F32)
            u = grad_in[at, :] * row_ref[at, 1:2] * lane_in[0:1, :]
            diff = u - m
            mean = jnp.sum(diff * diff, axis=1, keepdims=True) * (keep / (2 * ff))
            row_r = BETA_THREE * old[i * chunk : (i + 1) * chunk, 0:1] + (1.0 - BETA_THREE) * (
                mean + EPS_TWO
            )
            moment = BETA_ONE * m + (1.0 - BETA_ONE) * u
            new_w = w_in_ref[at, :].astype(F32) - moment * lax.rsqrt(row_r) * lane_in[1:2, :]
            for k in range(2):
                cols = slice(k * ff, (k + 1) * ff)
                new_m_in_ref[at, k, :] = moment[:, cols].astype(BF16)
                new_w_in_ref[at, k, :] = new_w[:, cols].astype(BF16)
            pieces.append(jnp.where(lane == 0, row_ref[at, 0:1], row_r))
        lanes = jnp.transpose(jnp.concatenate(pieces, axis=0))
        new_in_rows_ref[:, group * LANES : (group + 1) * LANES] = lanes[0:2, :]

    out_chunk = 32
    col_v = col_ref[0:1, :]
    col_scale = lax.rsqrt(col_v)
    for first in range(0, tile, LANES):
        cols = slice(first, first + LANES)
        scale = col_scale[:, cols]

        def res_body(i, carry):
            at = pl.ds(pl.multiple_of(i * out_chunk, out_chunk), out_chunk)
            m = m_out_ref[at, cols].astype(F32)
            u = grad_out[at, cols] * sub_out[0, at, :] * scale
            grad_out[at, cols] = u
            diff = u - m
            return carry + fold(diff * diff)

        res = lax.fori_loop(
            0, ff // out_chunk, res_body, jnp.zeros((8, LANES), F32), unroll=4
        )
        col_r = BETA_THREE * out_cols_ref[0, 1:2, cols] + (1.0 - BETA_THREE) * (
            jnp.sum(res, axis=0, keepdims=True) * (keep / ff) + EPS_TWO
        )
        col_step = lax.rsqrt(col_r)
        new_out_cols_ref[1:2, cols] = col_r

        def out_body(i, carry):
            at = pl.ds(pl.multiple_of(i * out_chunk, out_chunk), out_chunk)
            m = m_out_ref[at, cols].astype(F32)
            moment = BETA_ONE * m + (1.0 - BETA_ONE) * grad_out[at, cols]
            new_m_out_ref[at, cols] = moment.astype(BF16)
            new_w_out_ref[at, cols] = (
                w_out_ref[at, cols].astype(F32) - moment * sub_out[1, at, :] * col_step
            ).astype(BF16)
            return carry

        lax.fori_loop(0, ff // out_chunk, out_body, 0, unroll=4)
    new_out_cols_ref[0:1, :] = col_v


def per_device(
    tokens,
    cotangent,
    expert_ids,
    gate_logits,
    shadow_plan,
    w_in,
    w_out,
    mom_in,
    mom_out,
    in_rows,
    in_cols,
    out_rows,
    out_cols,
):
    groups = lax.axis_size("expert")
    fsdp_count = lax.axis_size("fsdp")
    fsdp_id = lax.axis_index("fsdp")
    tok_rows, topk_width = expert_ids.shape
    experts = shadow_plan.shape[0]
    feat = tokens.shape[1]
    ff = w_in.shape[3]
    full_rows = feat * fsdp_count
    capacity = tok_rows * topk_width // groups
    cores = 2 if groups % 2 == 0 else 1
    chips = groups // cores
    all_rows = groups * tok_rows
    half = all_rows // cores
    block = all_rows // fsdp_count
    w_in2 = w_in[0].reshape(feat, 2 * ff)
    m_in2 = mom_in[0].reshape(feat, 2 * ff)
    w_out2 = w_out[0]
    m_out2 = mom_out[0]
    lanes = -(-3 * experts // LANES) * LANES
    where = jnp.stack(
        [lax.axis_index("expert")]
        + [pairing(fsdp_count, d)[0](fsdp_id) for d in range(fsdp_count)]
        + [pairing(fsdp_count, d)[1](fsdp_id) for d in range(fsdp_count)]
    ).astype(jnp.int32)
    unit = all_rows * 3 * ff * 2
    limit = lambda count: pltpu.CompilerParams(vmem_limit_bytes=min(count, 40) * unit)

    def gather(value):
        pieces = [value] + [swap(value, "expert", groups, cores * d) for d in range(1, chips)]
        if cores == 1:
            return pieces
        return pieces + [swap(p, "expert", groups, 1) for p in pieces]

    def whole_specs(count):
        return [pl.BlockSpec()] * count

    anywhere = pl.BlockSpec(memory_space=pl.ANY)
    packed = pl.pallas_call(
        functools.partial(prep_kernel, capacity),
        in_specs=[SMEM] + [anywhere] * 3,
        out_specs=anywhere,
        out_shape=shape((tok_rows, feat + lanes), BF16),
        scratch_shapes=[
            pltpu.VMEM((topk_width, tok_rows), jnp.int32),
            pltpu.VMEM((topk_width, tok_rows), F32),
            pltpu.VMEM((tok_rows, lanes), BF16),
            pltpu.SemaphoreType.DMA((4,)),
        ],
        compiler_params=limit(3),
        name="prep",
    )(shadow_plan, expert_ids.T, gate_logits.T, cotangent)

    token_pieces = gather(tokens)
    rows_x, *pre = pl.pallas_call(
        functools.partial(forward_kernel, groups, fsdp_count),
        in_specs=[SMEM] + whole_specs(groups + 1),
        out_shape=[shape((all_rows, feat), BF16), shape((block, 2 * ff), F32)]
        + [shape((block, 2 * ff), BF16)] * (fsdp_count - 1),
        scratch_shapes=[pltpu.VMEM((all_rows, 2 * ff), F32)],
        compiler_params=limit(14),
        name="forward",
    )(where, *token_pieces, w_in2)
    pre = [pre[0]] + [swap(pre[d], "fsdp", fsdp_count, d) for d in range(1, fsdp_count)]

    packed_pieces = gather(packed)
    rows_o, gate, *hid = pl.pallas_call(
        functools.partial(backward_kernel, groups, fsdp_count, experts),
        in_specs=[SMEM] + whole_specs(groups + 1),
        out_shape=[
            shape((all_rows, feat), BF16),
            shape((all_rows, LANES), F32),
            shape((block, ff), F32),
        ]
        + [shape((block, ff), BF16)] * (fsdp_count - 1),
        scratch_shapes=[pltpu.VMEM((all_rows, ff), F32)],
        compiler_params=limit(12),
        name="backward",
    )(where, *packed_pieces, w_out2)
    hid = [hid[0]] + [swap(hid[d], "fsdp", fsdp_count, d) for d in range(1, fsdp_count)]
    made = pl.pallas_call(
        functools.partial(middle_kernel, fsdp_count),
        in_specs=whole_specs(2 * fsdp_count) + [pl.BlockSpec(memory_space=pl.ANY)],
        out_shape=shape((block, 3 * ff), BF16),
        compiler_params=limit(4),
        name="middle",
    )(*pre, *hid, m_in2)
    made = [made] + [swap(made, "fsdp", fsdp_count, d) for d in range(1, fsdp_count)]

    whole, *back = pl.pallas_call(
        functools.partial(output_kernel, fsdp_count, cores),
        in_specs=[SMEM] + whole_specs(3 + fsdp_count),
        out_shape=[shape((all_rows, 3 * ff), BF16)]
        + [shape((half, 2 * feat), F32)] * cores,
        compiler_params=limit(18),
        name="outputs",
    )(where, gate, w_in2, w_out2, *made)
    if cores == 2:
        got = swap(back[1], "expert", groups, 1)
        sums = pl.pallas_call(
            functools.partial(pair_kernel, chips),
            out_shape=[shape((tok_rows, 2 * feat), F32)]
            + [shape((tok_rows, 2 * feat), BF16)] * (chips - 1),
            compiler_params=limit(6),
            name="pair",
        )(back[0], got)
    else:
        sums = [back[0][d * tok_rows : (d + 1) * tok_rows] for d in range(chips)]
    sums = [sums[0]] + [swap(sums[d], "expert", groups, cores * d) for d in range(1, chips)]
    output, grad_tokens = pl.pallas_call(
        functools.partial(final_kernel, chips),
        out_shape=[shape((tok_rows, feat), BF16)] * 2,
        compiler_params=limit(3),
        name="final",
    )(*sums)

    tile = min(feat, 256)
    steps = feat // tile
    col_tile = lambda rows: pl.BlockSpec((rows, tile), lambda i: (0, i))
    row_tile = lambda cols: pl.BlockSpec((tile, cols), lambda i: (i, 0))
    full = lambda *dims: pl.BlockSpec(dims, lambda i: (0,) * len(dims))
    stats, row_state, col_state = pl.pallas_call(
        stats_kernel,
        grid=(steps,),
        in_specs=[
            col_tile(all_rows),
            full(all_rows, 3 * ff),
            col_tile(all_rows),
            row_tile(2 * ff),
            col_tile(ff),
            full(1, 2, feat),
            pl.BlockSpec((1, 2, tile), lambda i: (0, 0, i)),
        ],
        out_specs=[full(8, 3 * ff), row_tile(2), col_tile(8)],
        out_shape=[shape((8, 3 * ff), F32), shape((feat, 2), F32), shape((8, feat), F32)],
        scratch_shapes=[
            pltpu.VMEM((tile, 2 * ff), F32),
            pltpu.VMEM((ff, tile), F32),
            pltpu.VMEM((4, 8, 2 * ff), F32),
            pltpu.VMEM((4, ff, LANES), F32),
        ],
        compiler_params=limit(18),
        name="stats",
    )(rows_x, whole, rows_o, m_in2, m_out2, in_rows, out_cols)
    stats = [stats] + [swap(stats, "fsdp", fsdp_count, d) for d in range(1, fsdp_count)]

    new = pl.pallas_call(
        functools.partial(update_kernel, full_rows),
        grid=(steps,),
        in_specs=[
            col_tile(all_rows),
            full(all_rows, 3 * ff),
            col_tile(all_rows),
            row_tile(2 * ff),
            col_tile(ff),
            row_tile(2 * ff),
            col_tile(ff),
            pl.BlockSpec((1, 2, tile), lambda i: (0, 0, i)),
            full(1, 2, 2, ff),
            full(1, 2, ff),
            pl.BlockSpec((1, 2, tile), lambda i: (0, 0, i)),
            row_tile(2),
            col_tile(8),
        ]
        + [full(8, 3 * ff)] * fsdp_count,
        out_specs=[
            pl.BlockSpec((tile, 2, ff), lambda i: (i, 0, 0)),
            col_tile(ff),
            pl.BlockSpec((tile, 2, ff), lambda i: (i, 0, 0)),
            col_tile(ff),
            col_tile(2),
            full(2, 2, ff),
            full(2, ff),
            col_tile(2),
        ],
        out_shape=[
            shape((feat, 2, ff), BF16),
            shape((ff, feat), BF16),
            shape((feat, 2, ff), BF16),
            shape((ff, feat), BF16),
            shape((2, feat), F32),
            shape((2, 2, ff), F32),
            shape((2, ff), F32),
            shape((2, feat), F32),
        ],
        scratch_shapes=[
            pltpu.VMEM((tile, 2 * ff), F32),
            pltpu.VMEM((ff, tile), F32),
            pltpu.VMEM((8, 2 * ff), F32),
            pltpu.VMEM((2, ff, LANES), F32),
        ],
        compiler_params=limit(30),
        name="update",
    )(
        rows_x,
        whole,
        rows_o,
        m_in2,
        m_out2,
        w_in2,
        w_out2,
        in_rows,
        in_cols,
        out_rows,
        out_cols,
        row_state,
        col_state,
        *stats,
    )
    return (output, grad_tokens, *[value[None] for value in new])


def solution(mesh):
    return jax.shard_map(
        per_device,
        mesh=mesh,
        in_specs=(
            P("expert", "fsdp"),
            P("expert", "fsdp"),
            P("expert", None),
            P("expert", None),
            P(),
            P("expert", "fsdp", None, None),
            P("expert", None, "fsdp"),
            P("expert", "fsdp", None, None),
            P("expert", None, "fsdp"),
            P("expert", None, "fsdp"),
            P("expert", None, None, None),
            P("expert", None, None),
            P("expert", None, "fsdp"),
        ),
        out_specs=(
            P("expert", "fsdp"),
            P("expert", "fsdp"),
            P("expert", "fsdp", None, None),
            P("expert", None, "fsdp"),
            P("expert", "fsdp", None, None),
            P("expert", None, "fsdp"),
            P("expert", None, "fsdp"),
            P("expert", None, None, None),
            P("expert", None, None),
            P("expert", None, "fsdp"),
        ),
        check_vma=False,
    )
```

```python
import functools

import jax
import jax.numpy as jnp
from jax import lax
from jax.experimental import pallas as pl
from jax.experimental.pallas import tpu as pltpu
from jax.sharding import PartitionSpec as P


BETA_ONE = 0.9
BETA_TWO = 0.999
BETA_THREE = 0.9999
EPS_ONE = 1e-30
EPS_TWO = 1e-16
CLIP_LIMIT = 1.0
LEARN_RATE = 0.01
LANES = 128


F32 = jnp.float32
BF16 = jnp.bfloat16
SMEM = pl.BlockSpec(memory_space=pltpu.SMEM)


def pairing(count, step):
    if count & (count - 1) == 0:
        return lambda i: i ^ step, lambda i: i ^ step
    return lambda i: (i + step) % count, lambda i: (i - step) % count


def swap(value, axis, count, step):
    target, _ = pairing(count, step)
    return lax.ppermute(value, axis, [(i, target(i)) for i in range(count)])


def shape(dims, kind):
    return jax.ShapeDtypeStruct(dims, kind)


def dot_nt(a, b):
    return lax.dot_general(a, b, (((1,), (1,)), ((), ())), preferred_element_type=F32)


def dot_tn(a, b):
    return lax.dot_general(a, b, (((0,), (0,)), ((), ())), preferred_element_type=F32)


def prep_kernel(
    capacity,
    plan_hbm,
    ids_hbm,
    logits_hbm,
    cot_hbm,
    out_hbm,
    plan_ref,
    ids_ref,
    logits_ref,
    gate_ref,
    sems,
):
    choices, tok_rows = ids_ref.shape
    experts = plan_ref.shape[0]
    feat = cot_hbm.shape[1]
    lanes = gate_ref.shape[1]
    body = pltpu.make_async_copy(cot_hbm, out_hbm.at[:, pl.ds(0, feat)], sems.at[0])
    ids_copy = pltpu.make_async_copy(ids_hbm, ids_ref, sems.at[1])
    logits_copy = pltpu.make_async_copy(logits_hbm, logits_ref, sems.at[2])
    plan_copy = pltpu.make_async_copy(plan_hbm, plan_ref, sems.at[4])
    body.start()
    ids_copy.start()
    logits_copy.start()
    plan_copy.start()
    ids_copy.wait()
    logits_copy.wait()
    plan_copy.wait()
    sig = jax.nn.sigmoid(logits_ref[...])
    gates = sig / jnp.sum(sig, axis=0, keepdims=True)
    expert = lax.broadcasted_iota(jnp.int32, (experts, tok_rows), 0)
    present = jnp.zeros((experts, tok_rows), F32)
    weight = jnp.zeros((experts, tok_rows), F32)
    for k in range(choices):
        hit = ids_ref[k : k + 1, :] == expert
        present = present + jnp.where(hit, 1.0, 0.0)
        weight = weight + jnp.where(hit, gates[k : k + 1, :], 0.0)
    first = lax.broadcasted_iota(jnp.int32, (tok_rows, tok_rows), 0)
    second = lax.broadcasted_iota(jnp.int32, (tok_rows, tok_rows), 1)
    before = jnp.where(first < second, 1.0, 0.0).astype(BF16)
    rank = jnp.dot(present.astype(BF16), before, preferred_element_type=F32)
    limit = jnp.zeros((experts, tok_rows), jnp.int32)
    for e in range(experts):
        allowed = jnp.where(plan_ref[e] > 0, 2 * capacity, capacity)
        limit = jnp.where(expert == e, allowed, limit)
    limit = limit.astype(F32)
    weight = jnp.where((present > 0) & (rank < limit), weight, 0.0)
    high = weight.astype(BF16)
    rest = weight - high.astype(F32)
    middle = rest.astype(BF16)
    low = (rest - middle.astype(F32)).astype(BF16)
    stack = jnp.concatenate(
        [high.astype(F32), middle.astype(F32), low.astype(F32)]
        + ([jnp.zeros((lanes - 3 * experts, tok_rows), F32)] if lanes > 3 * experts else []),
        axis=0,
    )
    same = jnp.where(first == second, 1.0, 0.0).astype(BF16)
    gate_ref[...] = dot_nt(same, stack.astype(BF16)).astype(BF16)
    tail = pltpu.make_async_copy(gate_ref, out_hbm.at[:, pl.ds(feat, lanes)], sems.at[3])
    tail.start()
    tail.wait()
    body.wait()


def forward_kernel(pieces, blocks, where_ref, *refs):
    rows_in, w_ref = refs[:pieces], refs[pieces]
    rows_ref, own_ref = refs[pieces + 1 : pieces + 3]
    sends, part_ref = refs[pieces + 3 : -1], refs[-1]
    tok_rows = rows_in[0].shape[0]
    block = own_ref.shape[0]
    for k, ref in enumerate(rows_in):
        rows_ref[k * tok_rows : (k + 1) * tok_rows, :] = ref[...]
    part_ref[...] = jnp.dot(rows_ref[...], w_ref[...], preferred_element_type=F32)
    for d in range(blocks):
        start = pl.multiple_of(where_ref[1 + d] * block, block)
        piece = part_ref[pl.ds(start, block), :]
        if d == 0:
            own_ref[...] = piece
        else:
            sends[d - 1][...] = piece.astype(BF16)


def backward_kernel(pieces, blocks, experts, where_ref, *refs):
    packed, w_ref = refs[:pieces], refs[pieces]
    rows_ref, gate_ref, own_ref = refs[pieces + 1 : pieces + 4]
    sends, part_ref = refs[pieces + 4 : -1], refs[-1]
    tok_rows = packed[0].shape[0]
    feat = rows_ref.shape[1]
    block = own_ref.shape[0]
    lanes = packed[0].shape[1] - feat
    lane = lax.broadcasted_iota(jnp.int32, (tok_rows, lanes), 1)
    me = where_ref[0]
    mine = (lane == me) | (lane == me + experts) | (lane == me + 2 * experts)
    for k, ref in enumerate(packed):
        rows = slice(k * tok_rows, (k + 1) * tok_rows)
        parts = ref[:, feat:].astype(F32)
        gate = jnp.sum(jnp.where(mine, parts, 0.0), axis=1, keepdims=True)
        gate_ref[rows, :] = jnp.broadcast_to(gate, (tok_rows, LANES))
        rows_ref[rows, :] = (ref[:, :feat].astype(F32) * gate).astype(BF16)
    part_ref[...] = dot_nt(rows_ref[...], w_ref[...])
    for d in range(blocks):
        start = pl.multiple_of(where_ref[1 + d] * block, block)
        piece = part_ref[pl.ds(start, block), :]
        if d == 0:
            own_ref[...] = piece
        else:
            sends[d - 1][...] = piece.astype(BF16)


def middle_kernel(blocks, *refs):
    pre, grad, outs = refs[:blocks], refs[blocks : 2 * blocks], refs[2 * blocks + 1 :]
    ff = grad[0].shape[1]
    rows = outs[0].shape[0]
    step = 16

    def body(part, i, carry):
        at = pl.ds(pl.multiple_of(part * rows + i * step, step), step)
        to = pl.ds(pl.multiple_of(i * step, step), step)
        out_ref = outs[part]

        def total(parts, cols):
            value = parts[0][at, cols]
            for part in parts[1:]:
                value = value + part[at, cols].astype(F32)
            return value

        v = total(pre, slice(0, ff))
        w = total(pre, slice(ff, 2 * ff))
        g = total(grad, slice(0, ff))
        s = jax.nn.sigmoid(v)
        vs = v * s
        out_ref[to, 0:ff] = (vs * w).astype(BF16)
        out_ref[to, ff : 2 * ff] = (g * w * s * (1.0 + v * (1.0 - s))).astype(BF16)
        out_ref[to, 2 * ff : 3 * ff] = (g * vs).astype(BF16)
        return carry

    for part in range(len(outs)):
        lax.fori_loop(0, rows // step, functools.partial(body, part), 0)


def output_kernel(
    blocks, block, places, cores, where_ref, gate_ref, w_in_ref, w_out_ref, *refs
):
    pieces = refs[: len(places)]
    whole_ref, own_ref = refs[len(places) : len(places) + 2]
    ff = w_out_ref.shape[0]
    feat = w_out_ref.shape[1]
    half = own_ref.shape[0]
    for (d, offset), piece in zip(places, pieces):
        rows = piece.shape[0]
        start = pl.multiple_of(where_ref[1 + blocks + d] * block + offset, rows)
        whole_ref[pl.ds(start, rows), :] = piece[...]
    hidden = whole_ref[:, :ff]
    pre_grad = whole_ref[:, ff:]
    made = jnp.dot(hidden, w_out_ref[...], preferred_element_type=F32)
    made = made * gate_ref[:, :1]
    back = dot_nt(pre_grad, w_in_ref[...])
    own_ref[:, :feat] = made[:half]
    own_ref[:, feat:] = back[:half]
    if cores == 2:
        send_ref = refs[len(places) + 2]
        send_ref[:, :feat] = made[half:]
        send_ref[:, feat:] = back[half:]


def pair_kernel(chips, own_ref, got_ref, *outs):
    tok_rows = outs[0].shape[0]
    for d in range(chips):
        rows = slice(d * tok_rows, (d + 1) * tok_rows)
        outs[d][...] = (own_ref[rows, :] + got_ref[rows, :]).astype(outs[d].dtype)


def final_kernel(chips, *refs):
    parts, out_ref, grad_ref = refs[:chips], refs[chips], refs[chips + 1]
    feat = out_ref.shape[1]
    for ref, cols in ((out_ref, slice(0, feat)), (grad_ref, slice(feat, 2 * feat))):
        value = parts[0][:, cols]
        for part in parts[1:]:
            value = value + part[:, cols].astype(F32)
        ref[...] = value.astype(BF16)


def fold(value):
    rows, cols = value.shape
    return jnp.sum(value.reshape(rows // 8, 8, cols), axis=0)


def turned(row):
    return jnp.transpose(jnp.broadcast_to(row, (LANES, row.shape[1])))


def stats_kernel(
    rows_ref,
    whole_ref,
    out_grad_ref,
    m_in_ref,
    m_out_ref,
    in_rows_ref,
    out_cols_ref,
    stats_ref,
    row_ref,
    col_ref,
    grad_in,
    grad_out,
    acc_in,
    acc_out,
):
    step = pl.program_id(0)
    ff = whole_ref.shape[1] // 3
    tile = rows_ref.shape[1]

    @pl.when(step == 0)
    def _():
        acc_in[...] = jnp.zeros_like(acc_in)
        acc_out[...] = jnp.zeros_like(acc_out)

    grad_in[...] = dot_tn(rows_ref[...], whole_ref[:, ff:])
    grad_out[...] = dot_tn(whole_ref[:, :ff], out_grad_ref[...])
    chunk = 16

    def row_body(i, carry):
        at = pl.ds(pl.multiple_of(i * chunk, chunk), chunk)
        g = grad_in[at, :]
        row_ref[at, 0:1] = jnp.sum(g * g, axis=1, keepdims=True)
        return carry

    lax.fori_loop(0, tile // chunk, row_body, 0, unroll=True)
    mean = row_ref[:, 0:1] / (2 * ff)
    span = pl.ds(pl.multiple_of(step * tile, tile), tile)
    old = turned(in_rows_ref[0, 0:1, span])
    row_v = BETA_TWO * old[:, 0:1] + (1.0 - BETA_TWO) * (mean + EPS_ONE)
    row_ref[:, 0:1] = row_v
    row_ref[:, 1:2] = lax.rsqrt(row_v)
    slab = 4 * LANES
    for first in range(0, 2 * ff, slab):
        cols = slice(first, min(first + slab, 2 * ff))

        def in_body(i, carry):
            at = pl.ds(pl.multiple_of(i * chunk, chunk), chunk)
            g = grad_in[at, cols]
            m = m_in_ref[at, cols].astype(F32)
            h = g * row_ref[at, 1:2]
            parts = (g * g, h * h, h * m, m * m)
            return tuple(c + fold(p) for c, p in zip(carry, parts))

        zero = jnp.zeros((8, cols.stop - cols.start), F32)
        sums = lax.fori_loop(0, tile // chunk, in_body, (zero,) * 4, unroll=True)
        for k in range(4):
            acc_in[k, :, cols] += sums[k]
    out_chunk = 32

    def col_body(i, carry):
        at = pl.ds(pl.multiple_of(i * out_chunk, out_chunk), out_chunk)
        g = grad_out[at, :]
        return carry + fold(g * g)

    col_sq = lax.fori_loop(
        0, ff // out_chunk, col_body, jnp.zeros((8, tile), F32), unroll=True
    )
    col_v = BETA_TWO * out_cols_ref[0, 0:1, :] + (1.0 - BETA_TWO) * (
        jnp.sum(col_sq, axis=0, keepdims=True) / ff + EPS_ONE
    )
    col_ref[...] = jnp.broadcast_to(col_v, col_ref.shape)
    col_scale = lax.rsqrt(col_v)

    def squeeze(value):
        total = value[:, :LANES]
        for k in range(1, tile // LANES):
            total = total + value[:, k * LANES : (k + 1) * LANES]
        return total

    def out_body(i, carry):
        at = pl.ds(pl.multiple_of(i * out_chunk, out_chunk), out_chunk)
        g = grad_out[at, :]
        m = m_out_ref[at, :].astype(F32)
        h = g * col_scale
        acc_out[0, at, :] += squeeze(g * g)
        acc_out[1, at, :] += squeeze(h * h)
        acc_out[2, at, :] += squeeze(h * m)
        acc_out[3, at, :] += squeeze(m * m)
        return carry

    lax.fori_loop(0, ff // out_chunk, out_body, 0, unroll=True)

    @pl.when(step == pl.num_programs(0) - 1)
    def _():
        stats_ref[...] = jnp.zeros_like(stats_ref)
        for k in range(4):
            stats_ref[k : k + 1, : 2 * ff] = jnp.sum(acc_in[k], axis=0, keepdims=True)
            stats_ref[k : k + 1, 2 * ff :] = jnp.sum(
                jnp.transpose(acc_out[k]), axis=0, keepdims=True
            )
        for k in range(2):
            total = jnp.sum(in_rows_ref[0, k : k + 1, :], axis=1, keepdims=True)
            stats_ref[4 + k : 5 + k, :LANES] = jnp.broadcast_to(total, (1, LANES))


def update_kernel(
    full_rows,
    rows_ref,
    whole_ref,
    out_grad_ref,
    m_in_ref,
    m_out_ref,
    w_in_ref,
    w_out_ref,
    in_rows_ref,
    in_cols_ref,
    out_rows_ref,
    out_cols_ref,
    row_ref,
    col_ref,
    *refs,
):
    stats = refs[:-12]
    (
        new_w_in_ref,
        new_w_out_ref,
        new_m_in_ref,
        new_m_out_ref,
        new_in_rows_ref,
        new_in_cols_ref,
        new_out_rows_ref,
        new_out_cols_ref,
        grad_in,
        grad_out,
        lane_in,
        sub_out,
    ) = refs[-12:]
    ff = whole_ref.shape[1] // 3
    tile = rows_ref.shape[1]
    keep = BETA_ONE * BETA_ONE

    @pl.when(pl.program_id(0) == 0)
    def _():
        total = stats[0][...]
        for ref in stats[1:]:
            total = total + ref[...]
        col_sq, col_s, col_x, col_n = (total[k : k + 1, : 2 * ff] for k in range(4))
        row_sq, row_s, row_x, row_n = (total[k : k + 1, 2 * ff :] for k in range(4))
        sum_v = total[4:5, 0:1]
        sum_r = total[5:6, 0:1]
        count = full_rows * 2 * ff

        def over(value):
            return jnp.sum(value, axis=1, keepdims=True)

        def old_cols(which):
            return jnp.concatenate([in_cols_ref[0, which, k : k + 1, :] for k in range(2)], axis=1)

        col_v = BETA_TWO * old_cols(0) + (1.0 - BETA_TWO) * (
            col_sq / full_rows + EPS_ONE
        )
        row_v = BETA_TWO * out_rows_ref[0, 0:1, :] + (1.0 - BETA_TWO) * (
            row_sq / full_rows + EPS_ONE
        )
        mean_v_in = BETA_TWO * sum_v / full_rows + (1.0 - BETA_TWO) * (
            over(col_sq) / count + EPS_ONE
        )
        mean_v_out = over(row_v) / ff
        norm_in = mean_v_in * over(col_s / col_v) / count
        norm_out = mean_v_out * over(row_s / row_v) / (ff * full_rows)
        cb = (
            lax.rsqrt(col_v)
            * jnp.sqrt(mean_v_in)
            / jnp.maximum(1.0, jnp.sqrt(norm_in) / CLIP_LIMIT)
        )
        ra = (
            lax.rsqrt(row_v)
            * jnp.sqrt(mean_v_out)
            / jnp.maximum(1.0, jnp.sqrt(norm_out) / CLIP_LIMIT)
        )
        res_col = keep * (cb * (cb * col_s - 2.0 * col_x) + col_n)
        res_row = keep * (ra * (ra * row_s - 2.0 * row_x) + row_n)
        col_r = BETA_THREE * old_cols(1) + (1.0 - BETA_THREE) * (
            res_col / full_rows + EPS_TWO
        )
        row_r = BETA_THREE * out_rows_ref[0, 1:2, :] + (1.0 - BETA_THREE) * (
            res_row / full_rows + EPS_TWO
        )
        mean_r_in = BETA_THREE * sum_r / full_rows + (1.0 - BETA_THREE) * (
            over(res_col) / count + EPS_TWO
        )
        mean_r_out = over(row_r) / ff
        lane_in[0:1, :] = cb
        lane_in[1:2, :] = LEARN_RATE * jnp.sqrt(mean_r_in) * lax.rsqrt(col_r)
        step_row = LEARN_RATE * jnp.sqrt(mean_r_out) * lax.rsqrt(row_r)
        sub_out[0] = turned(ra)
        sub_out[1] = turned(step_row)
        for k in range(2):
            new_in_cols_ref[0, k : k + 1, :] = col_v[:, k * ff : (k + 1) * ff]
            new_in_cols_ref[1, k : k + 1, :] = col_r[:, k * ff : (k + 1) * ff]
        new_out_rows_ref[0:1, :] = row_v
        new_out_rows_ref[1:2, :] = row_r

    grad_in[...] = dot_tn(rows_ref[...], whole_ref[:, ff:])
    grad_out[...] = dot_tn(whole_ref[:, :ff], out_grad_ref[...])
    chunk = 16
    groups = tile // LANES
    for group in range(groups):
        lane = lax.broadcasted_iota(jnp.int32, (chunk, LANES), 1)
        pieces = []
        old = turned(in_rows_ref[0, 1:2, group * LANES : (group + 1) * LANES])
        for i in range(LANES // chunk):
            first = group * LANES + i * chunk
            at = slice(first, first + chunk)
            m = m_in_ref[at, :].astype(F32)
            u = grad_in[at, :] * row_ref[at, 1:2] * lane_in[0:1, :]
            diff = u - m
            mean = jnp.sum(diff * diff, axis=1, keepdims=True) * (keep / (2 * ff))
            row_r = BETA_THREE * old[i * chunk : (i + 1) * chunk, 0:1] + (1.0 - BETA_THREE) * (
                mean + EPS_TWO
            )
            moment = u - BETA_ONE * diff
            new_w = w_in_ref[at, :].astype(F32) - moment * lax.rsqrt(row_r) * lane_in[1:2, :]
            for k in range(2):
                cols = slice(k * ff, (k + 1) * ff)
                new_m_in_ref[at, k, :] = moment[:, cols].astype(BF16)
                new_w_in_ref[at, k, :] = new_w[:, cols].astype(BF16)
            pieces.append(jnp.where(lane == 0, row_ref[at, 0:1], row_r))
        lanes = jnp.transpose(jnp.concatenate(pieces, axis=0))
        new_in_rows_ref[:, group * LANES : (group + 1) * LANES] = lanes[0:2, :]

    out_chunk = 32
    col_v = col_ref[0:1, :]
    col_scale = lax.rsqrt(col_v)
    for first in range(0, tile, LANES):
        cols = slice(first, first + LANES)
        scale = col_scale[:, cols]

        def res_body(i, carry):
            at = pl.ds(pl.multiple_of(i * out_chunk, out_chunk), out_chunk)
            m = m_out_ref[at, cols].astype(F32)
            u = grad_out[at, cols] * sub_out[0, at, :] * scale
            grad_out[at, cols] = u
            diff = u - m
            return carry + fold(diff * diff)

        res = lax.fori_loop(
            0, ff // out_chunk, res_body, jnp.zeros((8, LANES), F32), unroll=True
        )
        col_r = BETA_THREE * out_cols_ref[0, 1:2, cols] + (1.0 - BETA_THREE) * (
            jnp.sum(res, axis=0, keepdims=True) * (keep / ff) + EPS_TWO
        )
        col_step = lax.rsqrt(col_r)
        new_out_cols_ref[1:2, cols] = col_r

        def out_body(i, carry):
            at = pl.ds(pl.multiple_of(i * out_chunk, out_chunk), out_chunk)
            m = m_out_ref[at, cols].astype(F32)
            moment = BETA_ONE * m + (1.0 - BETA_ONE) * grad_out[at, cols]
            new_m_out_ref[at, cols] = moment.astype(BF16)
            new_w_out_ref[at, cols] = (
                w_out_ref[at, cols].astype(F32) - moment * sub_out[1, at, :] * col_step
            ).astype(BF16)
            return carry

        lax.fori_loop(0, ff // out_chunk, out_body, 0, unroll=True)
    new_out_cols_ref[0:1, :] = col_v


def per_device(
    tokens,
    cotangent,
    expert_ids,
    gate_logits,
    shadow_plan,
    w_in,
    w_out,
    mom_in,
    mom_out,
    in_rows,
    in_cols,
    out_rows,
    out_cols,
):
    groups = lax.axis_size("expert")
    fsdp_count = lax.axis_size("fsdp")
    fsdp_id = lax.axis_index("fsdp")
    tok_rows, topk_width = expert_ids.shape
    experts = shadow_plan.shape[0]
    feat = tokens.shape[1]
    ff = w_in.shape[3]
    full_rows = feat * fsdp_count
    capacity = tok_rows * topk_width // groups
    cores = 2 if groups % 2 == 0 else 1
    chips = groups // cores
    all_rows = groups * tok_rows
    half = all_rows // cores
    block = all_rows // fsdp_count
    w_in2 = w_in[0].reshape(feat, 2 * ff)
    m_in2 = mom_in[0].reshape(feat, 2 * ff)
    w_out2 = w_out[0]
    m_out2 = mom_out[0]
    lanes = -(-3 * experts // LANES) * LANES
    where = jnp.stack(
        [lax.axis_index("expert")]
        + [pairing(fsdp_count, d)[0](fsdp_id) for d in range(fsdp_count)]
        + [pairing(fsdp_count, d)[1](fsdp_id) for d in range(fsdp_count)]
    ).astype(jnp.int32)
    unit = all_rows * 3 * ff * 2
    limit = lambda count: pltpu.CompilerParams(vmem_limit_bytes=min(count, 40) * unit)

    def gather(value):
        pieces = [value] + [swap(value, "expert", groups, cores * d) for d in range(1, chips)]
        if cores == 1:
            return pieces
        return pieces + [swap(p, "expert", groups, 1) for p in pieces]

    def whole_specs(count):
        return [pl.BlockSpec()] * count

    anywhere = pl.BlockSpec(memory_space=pltpu.HBM)
    far = lambda value: pltpu.with_memory_space_constraint(value, pltpu.HBM)
    packed = pl.pallas_call(
        functools.partial(prep_kernel, capacity),
        in_specs=[anywhere] * 4,
        out_specs=anywhere,
        out_shape=shape((tok_rows, feat + lanes), BF16),
        scratch_shapes=[
            pltpu.SMEM((experts,), jnp.int32),
            pltpu.VMEM((topk_width, tok_rows), jnp.int32),
            pltpu.VMEM((topk_width, tok_rows), F32),
            pltpu.VMEM((tok_rows, lanes), BF16),
            pltpu.SemaphoreType.DMA((5,)),
        ],
        compiler_params=limit(3),
        name="prep",
    )(far(shadow_plan), far(expert_ids.T), far(gate_logits.T), far(cotangent))

    token_pieces = gather(tokens)
    rows_x, *pre = pl.pallas_call(
        functools.partial(forward_kernel, groups, fsdp_count),
        in_specs=[SMEM] + whole_specs(groups + 1),
        out_shape=[shape((all_rows, feat), BF16), shape((block, 2 * ff), F32)]
        + [shape((block, 2 * ff), BF16)] * (fsdp_count - 1),
        scratch_shapes=[pltpu.VMEM((all_rows, 2 * ff), F32)],
        compiler_params=limit(14),
        name="forward",
    )(where, *token_pieces, w_in2)
    pre = [pre[0]] + [swap(pre[d], "fsdp", fsdp_count, d) for d in range(1, fsdp_count)]

    packed_pieces = gather(packed)
    rows_o, gate, *hid = pl.pallas_call(
        functools.partial(backward_kernel, groups, fsdp_count, experts),
        in_specs=[SMEM] + whole_specs(groups + 1),
        out_shape=[
            shape((all_rows, feat), BF16),
            shape((all_rows, LANES), F32),
            shape((block, ff), F32),
        ]
        + [shape((block, ff), BF16)] * (fsdp_count - 1),
        scratch_shapes=[pltpu.VMEM((all_rows, ff), F32)],
        compiler_params=limit(12),
        name="backward",
    )(where, *packed_pieces, w_out2)
    hid = [hid[0]] + [swap(hid[d], "fsdp", fsdp_count, d) for d in range(1, fsdp_count)]
    parts = 2 if fsdp_count == 4 else 1
    made = pl.pallas_call(
        functools.partial(middle_kernel, fsdp_count),
        in_specs=whole_specs(2 * fsdp_count) + [pl.BlockSpec(memory_space=pl.ANY)],
        out_shape=[shape((block // parts, 3 * ff), BF16)] * parts,
        compiler_params=limit(4),
        name="middle",
    )(*pre, *hid, m_in2)
    if parts == 2:
        first, second = made
        near_first = swap(first, "fsdp", fsdp_count, 1)
        side_second = swap(second, "fsdp", fsdp_count, 2)
        near_second = swap(second, "fsdp", fsdp_count, 1)
        side_first = swap(first, "fsdp", fsdp_count, 2)
        far_first = swap(near_first, "fsdp", fsdp_count, 2)
        far_second = swap(side_second, "fsdp", fsdp_count, 1)
        made = [
            first, second, near_first, near_second, side_first, side_second, far_first, far_second
        ]
        places = tuple((d, p * block // 2) for d in range(4) for p in range(2))
    else:
        made = [*made] + [swap(made[0], "fsdp", fsdp_count, d) for d in range(1, fsdp_count)]
        places = tuple((d, 0) for d in range(fsdp_count))

    whole, *back = pl.pallas_call(
        functools.partial(output_kernel, fsdp_count, block, places, cores),
        in_specs=[SMEM] + whole_specs(3 + len(made)),
        out_shape=[shape((all_rows, 3 * ff), BF16)]
        + [shape((half, 2 * feat), F32)] * cores,
        compiler_params=limit(18),
        name="outputs",
    )(where, gate, w_in2, w_out2, *made)
    if cores == 2:
        got = swap(back[1], "expert", groups, 1)
        sums = pl.pallas_call(
            functools.partial(pair_kernel, chips),
            out_shape=[shape((tok_rows, 2 * feat), F32)]
            + [shape((tok_rows, 2 * feat), BF16)] * (chips - 1),
            compiler_params=limit(6),
            name="pair",
        )(back[0], got)
    else:
        sums = [back[0][d * tok_rows : (d + 1) * tok_rows] for d in range(chips)]
    sums = [sums[0]] + [swap(sums[d], "expert", groups, cores * d) for d in range(1, chips)]
    output, grad_tokens = pl.pallas_call(
        functools.partial(final_kernel, chips),
        out_shape=[shape((tok_rows, feat), BF16)] * 2,
        compiler_params=limit(3),
        name="final",
    )(*sums)

    tile = min(feat, 512)
    steps = feat // tile
    col_tile = lambda rows: pl.BlockSpec((rows, tile), lambda i: (0, i))
    row_tile = lambda cols: pl.BlockSpec((tile, cols), lambda i: (i, 0))
    full = lambda *dims: pl.BlockSpec(dims, lambda i: (0,) * len(dims))
    stats, row_state, col_state = pl.pallas_call(
        stats_kernel,
        grid=(steps,),
        in_specs=[
            col_tile(all_rows),
            full(all_rows, 3 * ff),
            col_tile(all_rows),
            row_tile(2 * ff),
            col_tile(ff),
            full(1, 2, feat),
            pl.BlockSpec((1, 2, tile), lambda i: (0, 0, i)),
        ],
        out_specs=[full(8, 3 * ff), row_tile(2), col_tile(8)],
        out_shape=[shape((8, 3 * ff), F32), shape((feat, 2), F32), shape((8, feat), F32)],
        scratch_shapes=[
            pltpu.VMEM((tile, 2 * ff), F32),
            pltpu.VMEM((ff, tile), F32),
            pltpu.VMEM((4, 8, 2 * ff), F32),
            pltpu.VMEM((4, ff, LANES), F32),
        ],
        compiler_params=limit(18),
        name="stats",
    )(rows_x, whole, rows_o, m_in2, m_out2, in_rows, out_cols)
    stats = [stats] + [swap(stats, "fsdp", fsdp_count, d) for d in range(1, fsdp_count)]

    tile = min(feat, LANES)
    steps = feat // tile
    col_tile = lambda rows: pl.BlockSpec((rows, tile), lambda i: (0, i))
    row_tile = lambda cols: pl.BlockSpec((tile, cols), lambda i: (i, 0))
    new = pl.pallas_call(
        functools.partial(update_kernel, full_rows),
        grid=(steps,),
        in_specs=[
            col_tile(all_rows),
            full(all_rows, 3 * ff),
            col_tile(all_rows),
            row_tile(2 * ff),
            col_tile(ff),
            row_tile(2 * ff),
            col_tile(ff),
            pl.BlockSpec((1, 2, tile), lambda i: (0, 0, i)),
            full(1, 2, 2, ff),
            full(1, 2, ff),
            pl.BlockSpec((1, 2, tile), lambda i: (0, 0, i)),
            row_tile(2),
            col_tile(8),
        ]
        + [full(8, 3 * ff)] * fsdp_count,
        out_specs=[
            pl.BlockSpec((tile, 2, ff), lambda i: (i, 0, 0)),
            col_tile(ff),
            pl.BlockSpec((tile, 2, ff), lambda i: (i, 0, 0)),
            col_tile(ff),
            col_tile(2),
            full(2, 2, ff),
            full(2, ff),
            col_tile(2),
        ],
        out_shape=[
            shape((feat, 2, ff), BF16),
            shape((ff, feat), BF16),
            shape((feat, 2, ff), BF16),
            shape((ff, feat), BF16),
            shape((2, feat), F32),
            shape((2, 2, ff), F32),
            shape((2, ff), F32),
            shape((2, feat), F32),
        ],
        scratch_shapes=[
            pltpu.VMEM((tile, 2 * ff), F32),
            pltpu.VMEM((ff, tile), F32),
            pltpu.VMEM((8, 2 * ff), F32),
            pltpu.VMEM((2, ff, LANES), F32),
        ],
        compiler_params=limit(30),
        name="update",
    )(
        rows_x,
        whole,
        rows_o,
        m_in2,
        m_out2,
        w_in2,
        w_out2,
        in_rows,
        in_cols,
        out_rows,
        out_cols,
        row_state,
        col_state,
        *stats,
    )
    return (output, grad_tokens, *[value[None] for value in new])


def solution(mesh):
    return jax.shard_map(
        per_device,
        mesh=mesh,
        in_specs=(
            P("expert", "fsdp"),
            P("expert", "fsdp"),
            P("expert", None),
            P("expert", None),
            P(),
            P("expert", "fsdp", None, None),
            P("expert", None, "fsdp"),
            P("expert", "fsdp", None, None),
            P("expert", None, "fsdp"),
            P("expert", None, "fsdp"),
            P("expert", None, None, None),
            P("expert", None, None),
            P("expert", None, "fsdp"),
        ),
        out_specs=(
            P("expert", "fsdp"),
            P("expert", "fsdp"),
            P("expert", "fsdp", None, None),
            P("expert", None, "fsdp"),
            P("expert", "fsdp", None, None),
            P("expert", None, "fsdp"),
            P("expert", None, "fsdp"),
            P("expert", None, None, None),
            P("expert", None, None),
            P("expert", None, "fsdp"),
        ),
        check_vma=False,
    )
```
